512 devices in a mesh: seq: 32 (over z, core), img: 16 (over y, x).
Axes of the slice: x: 4, y: 4, z: 16, core: 2. Of those that a mesh axis runs over, the one named last changes fastest.
Arguments:
- tokens: bfloat16 [16, 96, 128, 2240], P('img', 'seq'), may hold values from -8 to 8
- norm_gain: bfloat16 [2240], replicated, may hold values from 0.099609375 to 1.8984375
- caption: bfloat16 [16, 2240], P('img'), may hold values from -6 to 6
- null_caption: bfloat16 [2240], replicated, may hold values from -6 to 6
- keep: int32 [16], P('img'), may hold values from 0 to 1, as said below
- bucket_rows: int32 [16], P('img'), may hold values from 25 to 96, as said below
- w_qkv: bfloat16 [2240, 3456], P('img', 'seq'), may hold values from -0.125 to 0.125
Outputs:
- attended: bfloat16 [16, 96, 128, 1152], P('img', 'seq')
The draws below stay inside these ranges and needn't reach their ends.
Inputs may be any that keep to these rules, and one draw needn't show every extreme that they name: `keep`: 1 keeps the image's caption, 0 drops it; some image keeps and some drops. `bucket_rows`: rows in use are the first ones of an image's grid; some image uses all 96 rows.
All inputs are finite; a program needn't handle non-finite values.
Results may differ from the reference program's by a relative error of at most 0.0017.
Values may be sent and summed in bfloat16 or wider, within the bound.
No kernel may reach another device: no remote copies, remote signals or barrier semaphores. Data moves between devices by JAX's collectives and lax.ppermute only.
A program may use at most 128 MiB of HBM per device.

```python
import jax
import jax.numpy as jnp
from jax import lax

D = 2240
HDIM = 32
HEADS = 36
WID = 128
INNER = 1152
HGT = 96
NIMG = 16


def draw_tokens(key, part):
    first, second = jax.random.split(key, 2)
    noise = jax.random.normal(first, (NIMG, HGT, WID, D), jnp.float32)
    means = jax.random.normal(second, (NIMG, HGT, 1, D), jnp.float32)
    values = noise + means
    return jnp.clip(values, -8.0, 8.0).astype(jnp.bfloat16)


def draw_keep(key, part):
    first, second = jax.random.split(jax.random.fold_in(key, 11))
    flags = jax.random.randint(first, (NIMG,), 0, 2)
    chosen = jax.random.randint(second, (), 0, NIMG)
    position = jnp.arange(NIMG, dtype=jnp.int32)
    flags = jnp.where(position == chosen, 1, flags)
    flags = jnp.where(position == (chosen + 1) % NIMG, 0, flags)
    return flags.astype(jnp.int32)


def draw_bucket_rows(key, part):
    first, second = jax.random.split(jax.random.fold_in(key, 23))
    lowest = HGT // 4 + 1
    heights = jax.random.randint(first, (NIMG,), lowest, HGT + 1)
    chosen = jax.random.randint(second, (), 0, NIMG)
    position = jnp.arange(NIMG, dtype=jnp.int32)
    heights = jnp.where(position == chosen, HGT, heights)
    heights = jnp.where(position == (chosen + 1) % NIMG, lowest, heights)
    return heights.astype(jnp.int32)


def block_levels(own_key, shape, shards, least, high):
    loudness = 1.0
    for axis_at, shards_of in shards:
        steps = jax.random.uniform(jax.random.fold_in(jax.random.fold_in(own_key, 6), axis_at), (shards_of,), jnp.float32, least / len(shards), high / len(shards))
        loudness = loudness * jnp.repeat(jnp.exp(steps), shape[axis_at] // shards_of).reshape((-1,) + (1,) * (len(shape) - 1 - axis_at))
    return loudness


def gaussian(stream_key, dims, scale, most, cuts=(), kind=jnp.bfloat16):
    values = scale * jax.random.normal(stream_key, dims, jnp.float32)
    if cuts:
        values = values * block_levels(stream_key, dims, cuts, -0.22, 0.18)
    return jnp.clip(values, -most, most).astype(kind)


def setup_inputs(seed: int = 0) -> dict:
    key_of = jax.random.split(jax.random.key(seed), 8)
    tokens = draw_tokens(jax.random.fold_in(key_of[7], 71), 0)
    norm_gain = jnp.clip(1.0 + 0.18 * jax.random.normal(key_of[1], (D,), jnp.float32), 0.099609375, 1.8984375).astype(jnp.bfloat16)
    caption = gaussian(key_of[2], (NIMG, D), 1.0, 6.0, ((0, 16),))
    null_caption = gaussian(key_of[3], (D,), 1.0, 6.0)
    keep = draw_keep(jax.random.fold_in(key_of[7], 71), 0)
    bucket_rows = draw_bucket_rows(jax.random.fold_in(key_of[7], 71), 0)
    w_qkv = gaussian(key_of[6], (D, 3 * INNER), D ** -0.5, 0.125, ((0, 16), (1, 32)))
    return dict(tokens=tokens, norm_gain=norm_gain, caption=caption, null_caption=null_caption, keep=keep, bucket_rows=bucket_rows, w_qkv=w_qkv)


norm_eps = 1e-06
attn_eps = 1e-06

def reference(tokens, norm_gain, caption, null_caption, keep, bucket_rows, w_qkv):
    inner_width = HEADS * HDIM
    token_count = HGT * WID

    def one_image(items):
        image, caption_row, keep_flag, height = items
        features = image.reshape(token_count, D).astype(jnp.float32)
        mean_square = lax.optimization_barrier(jnp.mean(features * features, axis=1, keepdims=True))
        condition = jnp.where(keep_flag > 0, caption_row, null_caption).astype(jnp.float32)
        hidden = (features * lax.rsqrt(mean_square + norm_eps) * norm_gain.astype(jnp.float32) + condition).astype(jnp.bfloat16)
        projected = jnp.dot(hidden, w_qkv, preferred_element_type=jnp.float32)
        grid_row = jnp.arange(token_count, dtype=jnp.int32) // WID
        live_mask = (grid_row < height).astype(jnp.float32)
        queries = jax.nn.relu(projected[:, :inner_width]).reshape(token_count, HEADS, HDIM)
        keys_relu = jax.nn.relu(projected[:, inner_width:2 * inner_width]).reshape(token_count, HEADS, HDIM)
        keys_relu = keys_relu * live_mask[:, None, None]
        values = projected[:, 2 * inner_width:].reshape(token_count, HEADS, HDIM)
        state_outer = jnp.einsum('thd,the->hde', keys_relu, values, precision=lax.Precision.HIGHEST)
        key_total = lax.optimization_barrier(jnp.sum(keys_relu, axis=0))
        numerator = jnp.einsum('thd,hde->the', queries, state_outer, precision=lax.Precision.HIGHEST)
        denominator = jnp.einsum('thd,hd->th', queries, key_total, precision=lax.Precision.HIGHEST)
        result = numerator / (denominator[:, :, None] + attn_eps) * live_mask[:, None, None]
        return result.reshape(HGT, WID, inner_width).astype(jnp.bfloat16)
    return lax.map(one_image, (tokens, caption, keep, bucket_rows))
```

```python
import functools

import jax
import jax.numpy as jnp
from jax import lax
from jax.experimental import pallas as pl
from jax.experimental.pallas import tpu as pltpu
from jax.sharding import PartitionSpec as P

HDIM = 32
LANES = 128
GROUP = LANES // HDIM

norm_eps = 1e-06
attn_eps = 1e-06
HIGHEST = lax.Precision.HIGHEST


def block_mask():
    row = lax.broadcasted_iota(jnp.int32, (LANES, LANES), 0) // HDIM
    col = lax.broadcasted_iota(jnp.int32, (LANES, LANES), 1) // HDIM
    return row == col


def live_rows(live_ref, tokens_per_core):
    token = lax.broadcasted_iota(jnp.int32, (2 * tokens_per_core, LANES), 0)
    limit = jnp.where(
        token < tokens_per_core, live_ref[0], live_ref[1] + tokens_per_core
    )
    return (token < limit).astype(jnp.float32)


def state_kernel(live_ref, mine_ref, other_ref, w_ref, out_ref, proj_ref):
    step = pl.program_id(0)
    tokens_per_core = mine_ref.shape[0]
    width = w_ref.shape[2]
    weights = w_ref[...].reshape(-1, width)
    at = pl.multiple_of(step * width, LANES)
    proj_ref[:tokens_per_core, pl.ds(at, width)] = jnp.dot(
        mine_ref[...], weights, preferred_element_type=jnp.float32
    )
    proj_ref[tokens_per_core:, pl.ds(at, width)] = jnp.dot(
        other_ref[...], weights, preferred_element_type=jnp.float32
    )

    @pl.when(step == pl.num_programs(0) - 1)
    def _():
        live = live_rows(live_ref, tokens_per_core)
        same_head = block_mask()
        full = proj_ref.shape[1] // LANES // 2
        chunks = out_ref.shape[0]
        rows = HDIM // chunks
        tiles = full + 1
        out_ref[...] = jnp.zeros_like(out_ref)
        for tile in range(tiles):
            if tile < full:
                keys = proj_ref[:, tile * LANES : (tile + 1) * LANES]
                values = proj_ref[:, (full + tile) * LANES : (full + tile + 1) * LANES]
                keep = same_head
            else:
                keys = proj_ref[:, 2 * full * LANES :]
                values = pltpu.roll(keys, LANES // 2, 1)
                half = lax.broadcasted_iota(jnp.int32, (LANES, LANES), 1) < LANES // 2
                keep = jnp.logical_and(same_head, half)
            keys = jnp.maximum(keys, 0.0) * live
            outer = lax.dot_general(
                keys,
                values,
                (((0,), (0,)), ((), ())),
                precision=HIGHEST,
                preferred_element_type=jnp.float32,
            )
            outer = jnp.where(keep, outer, 0.0)
            packed = outer[:HDIM]
            for head in range(1, GROUP):
                packed = packed + outer[head * HDIM : (head + 1) * HDIM]
            total = jnp.sum(keys, axis=0, keepdims=True)
            for chunk in range(chunks):
                for row in range(rows):
                    source = chunk * rows + row
                    target = row * tiles + tile
                    out_ref[chunk, target : target + 1, :] = packed[source : source + 1]
                target = rows * tiles + tile
                out_ref[chunk, target : target + 1, :] = total


def attend_kernel(live_ref, mine_ref, other_ref, w_ref, state_ref, own_ref, far_ref):
    tokens_per_core = mine_ref.shape[0]
    width = w_ref.shape[2]
    tiles = width // LANES
    chunks = state_ref.shape[0]
    rows = HDIM // chunks
    weights = w_ref[...].reshape(-1, width)
    live = live_rows(live_ref, tokens_per_core)
    same_head = block_mask()
    ones = same_head.astype(jnp.float32)
    for hidden_ref, result_ref, first in (
        (mine_ref, own_ref, 0),
        (other_ref, far_ref, tokens_per_core),
    ):
        queries = jnp.maximum(
            jnp.dot(hidden_ref[...], weights, preferred_element_type=jnp.float32), 0.0
        )
        for tile in range(tiles):
            query = queries[:, tile * LANES : (tile + 1) * LANES]
            packed = jnp.concatenate(
                [
                    state_ref[chunk, row * tiles + tile : row * tiles + tile + 1, :]
                    for chunk in range(chunks)
                    for row in range(rows)
                ],
                axis=0,
            )
            state = jnp.where(same_head, jnp.concatenate([packed] * GROUP, axis=0), 0.0)
            total = state_ref[0, rows * tiles + tile : rows * tiles + tile + 1, :]
            numerator = jnp.dot(
                query, state, precision=HIGHEST, preferred_element_type=jnp.float32
            )
            denominator = jnp.dot(
                query * total, ones, precision=HIGHEST, preferred_element_type=jnp.float32
            )
            result = numerator / (denominator + attn_eps)
            result = result * live[first : first + tokens_per_core]
            result_ref[:, tile * LANES : (tile + 1) * LANES] = result.astype(jnp.bfloat16)


def compute_state(live, mine, other, weights, chunks):
    images, depth, width = weights.shape
    tokens_per_core, contraction = mine.shape
    steps = 3
    block = width // steps
    tiles = width // LANES // 2 + 1
    slots = -(-(HDIM // chunks + 1) * tiles // 8) * 8
    whole = pl.BlockSpec((tokens_per_core, contraction), lambda i: (0, 0))
    return pl.pallas_call(
        state_kernel,
        grid=(steps,),
        in_specs=[
            pl.BlockSpec(memory_space=pltpu.SMEM),
            whole,
            whole,
            pl.BlockSpec((images, depth, block), lambda i: (0, 0, i)),
        ],
        out_specs=pl.BlockSpec((chunks, slots, LANES), lambda i: (0, 0, 0)),
        out_shape=jax.ShapeDtypeStruct((chunks, slots, LANES), jnp.float32),
        scratch_shapes=[pltpu.VMEM((2 * tokens_per_core, width), jnp.float32)],
        compiler_params=pltpu.CompilerParams(vmem_limit_bytes=48 * 1024 * 1024),
        name="state",
    )(live, mine, other, weights)


def compute_output(live, mine, other, weights, state):
    tokens_per_core = mine.shape[0]
    width = weights.shape[2]
    result = jax.ShapeDtypeStruct((tokens_per_core, width), jnp.bfloat16)
    vmem = pl.BlockSpec(memory_space=pltpu.VMEM)
    return pl.pallas_call(
        attend_kernel,
        in_specs=[pl.BlockSpec(memory_space=pltpu.SMEM), vmem, vmem, vmem, vmem],
        out_specs=[vmem, vmem],
        out_shape=[result, result],
        compiler_params=pltpu.CompilerParams(vmem_limit_bytes=48 * 1024 * 1024),
        name="attend",
    )(live, mine, other, weights, state)


def body(tokens, norm_gain, caption, null_caption, keep, bucket_rows, w_qkv):
    grid_rows, grid_cols, features_count = tokens.shape[1:]
    token_count = grid_rows * grid_cols
    seq_size = lax.axis_size("seq")
    img_size = lax.axis_size("img")
    chips = seq_size // 2
    seq_at = lax.axis_index("seq")
    core = seq_at % 2
    swap = [(s, s ^ 1) for s in range(seq_size)]
    same_core = [[2 * z + c for z in range(chips)] for c in range(2)]
    depth = features_count // img_size
    padded = -(-depth // 16) * 16
    columns = w_qkv.shape[1] * seq_size
    inner = columns // 3
    half = inner // 2
    main = half // LANES * LANES
    rest = half - main

    gathered = lax.all_gather(w_qkv, "seq", axis=0)
    rows = jnp.transpose(gathered, (1, 0, 2)).reshape(depth, columns)
    rows = jnp.pad(rows, ((0, padded - depth), (0, 0)))

    def pick(part):
        low = rows[:, part * inner : part * inner + half]
        high = rows[:, part * inner + half : (part + 1) * inner]
        return jnp.where(core == 0, low, high)

    query_cols, key_cols, value_cols = pick(0), pick(1), pick(2)
    pair = jnp.concatenate(
        [key_cols[:, :main], value_cols[:, :main], key_cols[:, main:], value_cols[:, main:]],
        axis=1,
    )
    query_cols = jnp.pad(query_cols, ((0, 0), (0, LANES - rest)))
    pair_weights = lax.all_gather(pair, "img", axis=0)
    query_weights = lax.all_gather(query_cols, "img", axis=0)

    features = jnp.transpose(tokens[0], (0, 2, 1)).astype(jnp.float32)
    mean_square = jnp.mean(features * features, axis=1, keepdims=True)
    condition = jnp.where(keep[0] > 0, caption[0], null_caption).astype(jnp.float32)
    hidden = (
        features * lax.rsqrt(mean_square + norm_eps) * norm_gain.astype(jnp.float32)[None, :, None]
        + condition[None, :, None]
    ).astype(jnp.bfloat16)
    hidden = hidden.reshape(grid_rows, img_size, depth, grid_cols)
    hidden = jnp.pad(hidden, ((0, 0), (0, 0), (0, padded - depth), (0, 0)))
    hidden = hidden.reshape(grid_rows, img_size * padded, grid_cols)
    mine = jnp.transpose(hidden, (0, 2, 1)).reshape(token_count, img_size * padded)
    other = lax.ppermute(mine, "seq", swap)

    first_row = jnp.stack([seq_at, seq_at ^ 1]) * grid_rows
    live = jnp.clip(bucket_rows[0] - first_row, 0, grid_rows) * grid_cols

    part = compute_state(live, mine, other, pair_weights, chips)
    part = lax.all_to_all(part, "seq", 0, 0, axis_index_groups=same_core)
    part = jnp.sum(part, axis=0)
    part = jnp.broadcast_to(part[None], (chips,) + part.shape)
    state = lax.all_to_all(part, "seq", 0, 0, axis_index_groups=same_core)

    own, far = compute_output(live, mine, other, query_weights, state)
    back = lax.ppermute(far, "seq", swap)
    own, back = own[:, :half], back[:, :half]
    result = jnp.where(
        core == 0,
        jnp.concatenate([own, back], axis=1),
        jnp.concatenate([back, own], axis=1),
    )
    return result.reshape(1, grid_rows, grid_cols, inner)


def solution(mesh):
    in_specs = (
        P("img", "seq", None, None),
        P(),
        P("img", None),
        P(),
        P("img"),
        P("img"),
        P("img", "seq"),
    )
    out_specs = P("img", "seq", None, None)
    return jax.shard_map(body, mesh=mesh, in_specs=in_specs, out_specs=out_specs, check_vma=False)
```

```python
import functools

import jax
import jax.numpy as jnp
from jax import lax
from jax.experimental import pallas as pl
from jax.experimental.pallas import tpu as pltpu
from jax.sharding import PartitionSpec as P

HDIM = 32
LANES = 128
GROUP = LANES // HDIM

norm_eps = 1e-06
attn_eps = 1e-06
HIGHEST = lax.Precision.HIGHEST


def block_mask():
    row = lax.broadcasted_iota(jnp.int32, (LANES, LANES), 0) // HDIM
    col = lax.broadcasted_iota(jnp.int32, (LANES, LANES), 1) // HDIM
    return row == col


def live_rows(live_ref, tokens_per_core):
    token = lax.broadcasted_iota(jnp.int32, (2 * tokens_per_core, LANES), 0)
    limit = jnp.where(
        token < tokens_per_core, live_ref[0], live_ref[1] + tokens_per_core
    )
    return (token < limit).astype(jnp.float32)


def stack_blocks(pieces, masks, start, width):
    blocks = {}
    for piece, held in zip(pieces, masks):
        for at, mask in enumerate(held):
            blocks[mask] = piece[at, :, start : start + width]
    return jnp.concatenate([blocks[mask] for mask in sorted(blocks)], axis=0)


def project(hidden_refs, pieces, masks, start, width):
    weights = stack_blocks(pieces, masks, start, width)
    return jnp.concatenate(
        [
            jnp.dot(ref[...], weights, preferred_element_type=jnp.float32)
            for ref in hidden_refs
        ],
        axis=0,
    )


def state_kernel(masks, full, *refs):
    count = len(masks[0])
    live_ref, mine_ref, other_ref = refs[:3]
    first, second = refs[3 : 3 + count], refs[3 + count : 3 + 2 * count]
    out_ref, keys_ref, values_ref = refs[3 + 2 * count :]
    hidden = (mine_ref, other_ref)
    step = 2 * LANES
    for start in range(0, (full + 1) * LANES, step):
        width = min(step, (full + 1) * LANES - start)
        keys_ref[:, start : start + width] = project(hidden, first, masks[0], start, width)
    for start in range(0, full * LANES, step):
        values_ref[:, start : start + step] = project(hidden, second, masks[1], start, step)
    live = live_rows(live_ref, mine_ref.shape[0])
    same_head = block_mask()
    chunks = out_ref.shape[0]
    rows = HDIM // chunks
    tiles = full + 1
    out_ref[...] = jnp.zeros_like(out_ref)
    for tile in range(tiles):
        keys = keys_ref[:, tile * LANES : (tile + 1) * LANES]
        if tile < full:
            values = values_ref[:, tile * LANES : (tile + 1) * LANES]
            keep = same_head
        else:
            values = pltpu.roll(keys, LANES // 2, 1)
            half = lax.broadcasted_iota(jnp.int32, (LANES, LANES), 1) < LANES // 2
            keep = jnp.logical_and(same_head, half)
        keys = jnp.maximum(keys, 0.0) * live
        outer = lax.dot_general(
            keys,
            values,
            (((0,), (0,)), ((), ())),
            precision=HIGHEST,
            preferred_element_type=jnp.float32,
        )
        outer = jnp.where(keep, outer, 0.0)
        packed = outer[:HDIM]
        for head in range(1, GROUP):
            packed = packed + outer[head * HDIM : (head + 1) * HDIM]
        total = jnp.sum(keys, axis=0, keepdims=True)
        for chunk in range(chunks):
            for row in range(rows):
                source = chunk * rows + row
                target = row * tiles + tile
                out_ref[chunk, target : target + 1, :] = packed[source : source + 1]
            target = rows * tiles + tile
            out_ref[chunk, target : target + 1, :] = total


def query_kernel(masks, full, *refs):
    count = len(masks[0])
    hidden = refs[:2]
    first, second = refs[2 : 2 + count], refs[2 + count : 2 + 2 * count]
    out_ref = refs[2 + 2 * count]
    width = first[0].shape[2]
    at = 0
    for pieces, held, start in (
        (first, masks[0], (full + 1) * LANES),
        (second, masks[1], full * LANES),
    ):
        size = width - start
        out_ref[:, at : at + size] = jnp.maximum(
            project(hidden, pieces, held, start, size), 0.0
        )
        at += size


def attend_kernel(live_ref, query_ref, state_ref, own_ref, far_ref):
    tokens_per_core = own_ref.shape[0]
    tiles = query_ref.shape[1] // LANES
    chunks = state_ref.shape[0]
    rows = HDIM // chunks
    live = live_rows(live_ref, tokens_per_core)
    same_head = block_mask()
    ones = same_head.astype(jnp.float32)
    for tile in range(tiles):
        query = query_ref[:, tile * LANES : (tile + 1) * LANES]
        packed = jnp.concatenate(
            [
                state_ref[chunk, row * tiles + tile : row * tiles + tile + 1, :]
                for chunk in range(chunks)
                for row in range(rows)
            ],
            axis=0,
        )
        state = jnp.where(same_head, jnp.concatenate([packed] * GROUP, axis=0), 0.0)
        total = state_ref[0, rows * tiles + tile : rows * tiles + tile + 1, :]
        numerator = jnp.dot(
            query, state, precision=HIGHEST, preferred_element_type=jnp.float32
        )
        denominator = jnp.dot(
            query * total, ones, precision=HIGHEST, preferred_element_type=jnp.float32
        )
        result = (numerator / (denominator + attn_eps) * live).astype(jnp.bfloat16)
        own_ref[:, tile * LANES : (tile + 1) * LANES] = result[:tokens_per_core]
        far_ref[:, tile * LANES : (tile + 1) * LANES] = result[tokens_per_core:]


VMEM = pl.BlockSpec(memory_space=pltpu.VMEM)
SMEM = pl.BlockSpec(memory_space=pltpu.SMEM)
PARAMS = pltpu.CompilerParams(vmem_limit_bytes=24 * 1024 * 1024)


def compute_state(live, hidden, first, second, masks, full, chunks):
    tokens = 2 * hidden[0].shape[0]
    slots = -(-(HDIM // chunks + 1) * (full + 1) // 8) * 8
    return pl.pallas_call(
        functools.partial(state_kernel, masks, full),
        in_specs=[SMEM] + [VMEM] * (2 + len(first) + len(second)),
        out_specs=VMEM,
        out_shape=jax.ShapeDtypeStruct((chunks, slots, LANES), jnp.float32),
        scratch_shapes=[
            pltpu.VMEM((tokens, (full + 1) * LANES), jnp.float32),
            pltpu.VMEM((tokens, full * LANES), jnp.float32),
        ],
        compiler_params=PARAMS,
        name="state",
    )(live, *hidden, *first, *second)


def compute_queries(hidden, first, second, masks, full):
    tokens = 2 * hidden[0].shape[0]
    contraction = hidden[0].shape[1]
    width = 2 * first[0].shape[2] - (2 * full + 1) * LANES
    return pl.pallas_call(
        functools.partial(query_kernel, masks, full),
        in_specs=[VMEM] * (2 + len(first) + len(second)),
        out_specs=VMEM,
        out_shape=jax.ShapeDtypeStruct((tokens, width), jnp.float32),
        compiler_params=PARAMS,
        cost_estimate=pl.CostEstimate(
            flops=2 * tokens * contraction * width,
            bytes_accessed=4 * tokens * width + 2 * contraction * width,
            transcendentals=0,
        ),
        name="queries",
    )(*hidden, *first, *second)


def compute_output(live, queries, state):
    tokens, width = queries.shape
    result = jax.ShapeDtypeStruct((tokens // 2, width), jnp.bfloat16)
    return pl.pallas_call(
        attend_kernel,
        in_specs=[SMEM, VMEM, VMEM],
        out_specs=[VMEM, VMEM],
        out_shape=[result, result],
        compiler_params=pltpu.CompilerParams(vmem_limit_bytes=12 * 1024 * 1024),
        name="attend",
    )(live, queries, state)


def reorder_kernel(order_ref, source_ref, out_ref):
    for at in range(out_ref.shape[1]):
        out_ref[:, at] = source_ref[:, order_ref[at]]


def exchange(block, mask, count):
    return lax.ppermute(block, "img", [(i, i ^ mask) for i in range(count)])


def near_stage(block, masks, count):
    held, names = block[None], [0]
    for mask in masks:
        held = jnp.concatenate([held, exchange(held, mask, count)], axis=0)
        names = names + [name ^ mask for name in names]
    return held, names


def far_stage(held, names, masks, count):
    middle = held.shape[0] // 2
    pieces, labels = [held], [names]
    for half, label, order in (
        (held[:middle], names[:middle], masks),
        (held[middle:], names[middle:], masks[::-1]),
    ):
        near = exchange(half, order[0], count)
        near_label = [name ^ order[0] for name in label]
        both = jnp.concatenate([half, near], axis=0)
        far = exchange(both, order[1], count)
        pieces += [near, far]
        labels += [near_label, [name ^ order[1] for name in label + near_label]]
    return pieces, labels


def body(tokens, norm_gain, caption, null_caption, keep, bucket_rows, w_qkv):
    grid_rows, grid_cols, features_count = tokens.shape[1:]
    token_count = grid_rows * grid_cols
    seq_size = lax.axis_size("seq")
    img_size = lax.axis_size("img")
    chips = seq_size // 2
    seq_at = lax.axis_index("seq")
    core = seq_at % 2
    swap = [(s, s ^ 1) for s in range(seq_size)]
    same_core = [[2 * z + c for z in range(chips)] for c in range(2)]
    depth = features_count // img_size
    padded = -(-depth // 16) * 16
    columns = w_qkv.shape[1] * seq_size
    inner = columns // 3
    half = inner // 2
    main = half // LANES * LANES
    rest = half - main

    gathered = lax.all_gather(w_qkv, "seq", axis=0)
    rows = jnp.transpose(gathered, (1, 0, 2)).reshape(depth, columns)
    rows = jnp.pad(rows, ((0, padded - depth), (0, 0)))

    def pick(part):
        low = rows[:, part * inner : part * inner + half]
        high = rows[:, part * inner + half : (part + 1) * inner]
        return jnp.where(core == 0, low, high)

    query_cols, key_cols, value_cols = pick(0), pick(1), pick(2)
    full = main // LANES
    split = main // 2
    first = jnp.concatenate(
        [key_cols, value_cols[:, main:], query_cols[:, :split]], axis=1
    )
    second = jnp.concatenate(
        [value_cols[:, :main], jnp.pad(query_cols[:, split:], ((0, 0), (0, LANES - rest)))],
        axis=1,
    )
    across, along = (1, 3), (4, 12)
    first_near, first_names = near_stage(first, across, img_size)
    second_near, second_names = near_stage(second, along, img_size)
    first_pieces, first_masks = far_stage(first_near, first_names, along, img_size)
    second_pieces, second_masks = far_stage(second_near, second_names, across, img_size)
    masks = (first_masks, second_masks)

    features = jnp.transpose(tokens[0], (0, 2, 1)).astype(jnp.float32)
    mean_square = jnp.mean(features * features, axis=1, keepdims=True)
    condition = jnp.where(keep[0] > 0, caption[0], null_caption).astype(jnp.float32)
    hidden = (
        features * lax.rsqrt(mean_square + norm_eps) * norm_gain.astype(jnp.float32)[None, :, None]
        + condition[None, :, None]
    ).astype(jnp.bfloat16)
    hidden = hidden.reshape(grid_rows, img_size, depth, grid_cols)
    hidden = jnp.pad(hidden, ((0, 0), (0, 0), (0, padded - depth), (0, 0)))
    order = jnp.bitwise_xor(lax.axis_index("img"), jnp.arange(img_size, dtype=jnp.int32))
    hidden = pl.pallas_call(
        reorder_kernel,
        in_specs=[SMEM, VMEM],
        out_specs=VMEM,
        out_shape=jax.ShapeDtypeStruct(hidden.shape, hidden.dtype),
        compiler_params=pltpu.CompilerParams(vmem_limit_bytes=8 * 1024 * 1024),
        name="reorder",
    )(order, hidden)
    hidden = hidden.reshape(grid_rows, img_size * padded, grid_cols)
    mine = jnp.transpose(hidden, (0, 2, 1)).reshape(token_count, img_size * padded)
    other = lax.ppermute(mine, "seq", swap)

    first_row = jnp.stack([seq_at, seq_at ^ 1]) * grid_rows
    live = jnp.clip(bucket_rows[0] - first_row, 0, grid_rows) * grid_cols

    part = compute_state(live, (mine, other), first_pieces, second_pieces, masks, full, chips)
    part = lax.all_to_all(part, "seq", 0, 0, axis_index_groups=same_core)
    queries = compute_queries((mine, other), first_pieces, second_pieces, masks, full)
    part = jnp.sum(part, axis=0)
    part = jnp.broadcast_to(part[None], (chips,) + part.shape)
    state = lax.all_to_all(part, "seq", 0, 0, axis_index_groups=same_core)

    own, far = compute_output(live, queries, state)
    back = lax.ppermute(far, "seq", swap)
    own, back = own[:, :half], back[:, :half]
    result = jnp.where(
        core == 0,
        jnp.concatenate([own, back], axis=1),
        jnp.concatenate([back, own], axis=1),
    )
    return result.reshape(1, grid_rows, grid_cols, inner)


def solution(mesh):
    in_specs = (
        P("img", "seq", None, None),
        P(),
        P("img", None),
        P(),
        P("img"),
        P("img"),
        P("img", "seq"),
    )
    out_specs = P("img", "seq", None, None)
    return jax.shard_map(body, mesh=mesh, in_specs=in_specs, out_specs=out_specs, check_vma=False)
```

```python
import functools

import jax
import jax.numpy as jnp
from jax import lax
from jax.experimental import pallas as pl
from jax.experimental.pallas import tpu as pltpu
from jax.sharding import PartitionSpec as P

HDIM = 32
LANES = 128
GROUP = LANES // HDIM

norm_eps = 1e-06
attn_eps = 1e-06
HIGHEST = lax.Precision.HIGHEST


def block_mask():
    row = lax.broadcasted_iota(jnp.int32, (LANES, LANES), 0) // HDIM
    col = lax.broadcasted_iota(jnp.int32, (LANES, LANES), 1) // HDIM
    return row == col


def live_rows(live_ref, tokens_per_core):
    token = lax.broadcasted_iota(jnp.int32, (2 * tokens_per_core, LANES), 0)
    limit = jnp.where(
        token < tokens_per_core, live_ref[0], live_ref[1] + tokens_per_core
    )
    return (token < limit).astype(jnp.float32)


def load_blocks(pieces, masks, start, into_ref, sems):
    depth, width = pieces[0].shape[1], into_ref.shape[1]
    copies = []
    for piece, held in zip(pieces, masks):
        for at, mask in enumerate(held):
            copies.append(
                pltpu.make_async_copy(
                    piece.at[at, :, pl.ds(start, width)],
                    into_ref.at[pl.ds(mask * depth, depth), :],
                    sems.at[len(copies)],
                )
            )
    for copy in copies:
        copy.start()
    return copies


def project(hidden, copies, weights_ref, out_ref, at):
    for copy in copies:
        copy.wait()
    tokens = hidden[0].shape[0]
    step = 2 * LANES
    for start in range(0, weights_ref.shape[1], step):
        width = min(step, weights_ref.shape[1] - start)
        weights = weights_ref[:, start : start + width]
        for row, ref in enumerate(hidden):
            out_ref[row * tokens : (row + 1) * tokens, at + start : at + start + width] = jnp.dot(
                ref[...], weights, preferred_element_type=jnp.float32
            )


def state_kernel(masks, full, *refs):
    count = len(masks[0])
    live_ref, mine_ref, other_ref = refs[:3]
    first, second = refs[3 : 3 + count], refs[3 + count : 3 + 2 * count]
    out_ref, keys_ref, values_ref, key_w, value_w, key_sems, value_sems = refs[3 + 2 * count :]
    hidden = (mine_ref, other_ref)
    key_copies = load_blocks(first, masks[0], 0, key_w, key_sems)
    value_copies = load_blocks(second, masks[1], 0, value_w, value_sems)
    project(hidden, key_copies, key_w, keys_ref, 0)
    project(hidden, value_copies, value_w, values_ref, 0)
    live = live_rows(live_ref, mine_ref.shape[0])
    same_head = block_mask()
    chunks = out_ref.shape[0]
    rows = HDIM // chunks
    tiles = full + 1
    out_ref[...] = jnp.zeros_like(out_ref)
    for tile in range(tiles):
        keys = keys_ref[:, tile * LANES : (tile + 1) * LANES]
        if tile < full:
            values = values_ref[:, tile * LANES : (tile + 1) * LANES]
            keep = same_head
        else:
            values = pltpu.roll(keys, LANES // 2, 1)
            half = lax.broadcasted_iota(jnp.int32, (LANES, LANES), 1) < LANES // 2
            keep = jnp.logical_and(same_head, half)
        keys = jnp.maximum(keys, 0.0) * live
        outer = lax.dot_general(
            keys,
            values,
            (((0,), (0,)), ((), ())),
            precision=HIGHEST,
            preferred_element_type=jnp.float32,
        )
        outer = jnp.where(keep, outer, 0.0)
        packed = outer[:HDIM]
        for head in range(1, GROUP):
            packed = packed + outer[head * HDIM : (head + 1) * HDIM]
        total = jnp.sum(keys, axis=0, keepdims=True)
        for chunk in range(chunks):
            for row in range(rows):
                source = chunk * rows + row
                target = row * tiles + tile
                out_ref[chunk, target : target + 1, :] = packed[source : source + 1]
            target = rows * tiles + tile
            out_ref[chunk, target : target + 1, :] = total


def query_kernel(masks, full, *refs):
    count = len(masks[0])
    hidden = refs[:2]
    first, second = refs[2 : 2 + count], refs[2 + count : 2 + 2 * count]
    out_ref, low_w, high_w, low_sems, high_sems = refs[2 + 2 * count :]
    low_copies = load_blocks(first, masks[0], (full + 1) * LANES, low_w, low_sems)
    high_copies = load_blocks(second, masks[1], full * LANES, high_w, high_sems)
    project(hidden, low_copies, low_w, out_ref, 0)
    project(hidden, high_copies, high_w, out_ref, low_w.shape[1])


def attend_kernel(live_ref, query_ref, state_ref, own_ref, far_ref):
    tokens_per_core = own_ref.shape[0]
    tiles = query_ref.shape[1] // LANES
    chunks = state_ref.shape[0]
    rows = HDIM // chunks
    live = live_rows(live_ref, tokens_per_core)
    same_head = block_mask()
    ones = same_head.astype(jnp.float32)
    for tile in range(tiles):
        query = jnp.maximum(query_ref[:, tile * LANES : (tile + 1) * LANES], 0.0)
        packed = jnp.concatenate(
            [
                state_ref[chunk, row * tiles + tile : row * tiles + tile + 1, :]
                for chunk in range(chunks)
                for row in range(rows)
            ],
            axis=0,
        )
        state = jnp.where(same_head, jnp.concatenate([packed] * GROUP, axis=0), 0.0)
        total = state_ref[0, rows * tiles + tile : rows * tiles + tile + 1, :]
        numerator = jnp.dot(
            query, state, precision=HIGHEST, preferred_element_type=jnp.float32
        )
        denominator = jnp.dot(
            query * total, ones, precision=HIGHEST, preferred_element_type=jnp.float32
        )
        result = (numerator / (denominator + attn_eps) * live).astype(jnp.bfloat16)
        own_ref[:, tile * LANES : (tile + 1) * LANES] = result[:tokens_per_core]
        far_ref[:, tile * LANES : (tile + 1) * LANES] = result[tokens_per_core:]


VMEM = pl.BlockSpec(memory_space=pltpu.VMEM)
SMEM = pl.BlockSpec(memory_space=pltpu.SMEM)
ANY = pl.BlockSpec(memory_space=pltpu.HBM)
PARAMS = pltpu.CompilerParams(vmem_limit_bytes=58 * 1024 * 1024)


def compute_state(live, hidden, first, second, masks, full, chunks):
    tokens = 2 * hidden[0].shape[0]
    contraction = hidden[0].shape[1]
    slots = -(-(HDIM // chunks + 1) * (full + 1) // 8) * 8
    return pl.pallas_call(
        functools.partial(state_kernel, masks, full),
        in_specs=[SMEM] + [VMEM] * 2 + [ANY] * (len(first) + len(second)),
        out_specs=VMEM,
        out_shape=jax.ShapeDtypeStruct((chunks, slots, LANES), jnp.float32),
        scratch_shapes=[
            pltpu.VMEM((tokens, (full + 1) * LANES), jnp.float32),
            pltpu.VMEM((tokens, full * LANES), jnp.float32),
            pltpu.VMEM((contraction, (full + 1) * LANES), jnp.bfloat16),
            pltpu.VMEM((contraction, full * LANES), jnp.bfloat16),
            pltpu.SemaphoreType.DMA((contraction // first[0].shape[1],)),
            pltpu.SemaphoreType.DMA((contraction // first[0].shape[1],)),
        ],
        compiler_params=PARAMS,
        name="state",
    )(live, *hidden, *first, *second)


def compute_queries(hidden, first, second, masks, full):
    tokens = 2 * hidden[0].shape[0]
    contraction = hidden[0].shape[1]
    low = first[0].shape[2] - (full + 1) * LANES
    width = low + second[0].shape[2] - full * LANES
    return pl.pallas_call(
        functools.partial(query_kernel, masks, full),
        in_specs=[VMEM] * 2 + [ANY] * (len(first) + len(second)),
        out_specs=VMEM,
        out_shape=jax.ShapeDtypeStruct((tokens, width), jnp.float32),
        scratch_shapes=[
            pltpu.VMEM((contraction, low), jnp.bfloat16),
            pltpu.VMEM((contraction, width - low), jnp.bfloat16),
            pltpu.SemaphoreType.DMA((contraction // first[0].shape[1],)),
            pltpu.SemaphoreType.DMA((contraction // first[0].shape[1],)),
        ],
        compiler_params=PARAMS,
        cost_estimate=pl.CostEstimate(
            flops=2 * tokens * contraction * width,
            bytes_accessed=4 * tokens * width + 2 * contraction * width,
            transcendentals=0,
        ),
        name="queries",
    )(*hidden, *first, *second)


def compute_output(live, queries, state):
    tokens, width = queries.shape
    result = jax.ShapeDtypeStruct((tokens // 2, width), jnp.bfloat16)
    return pl.pallas_call(
        attend_kernel,
        in_specs=[SMEM, VMEM, VMEM],
        out_specs=[VMEM, VMEM],
        out_shape=[result, result],
        compiler_params=pltpu.CompilerParams(vmem_limit_bytes=58 * 1024 * 1024),
        name="attend",
    )(live, queries, state)


def reorder_kernel(order_ref, source_ref, out_ref):
    for at in range(out_ref.shape[1]):
        out_ref[:, at] = source_ref[:, order_ref[at]]


def exchange(block, mask, count):
    return lax.ppermute(block, "img", [(i, i ^ mask) for i in range(count)])


def near_stage(block, masks, count):
    held, names = block[None], [0]
    for mask in masks:
        held = jnp.concatenate([held, exchange(held, mask, count)], axis=0)
        names = names + [name ^ mask for name in names]
    return held, names


def far_stage(held, names, masks, count):
    middle = held.shape[0] // 2
    one, two = masks
    from_one = exchange(held, one, count)
    from_two = exchange(held, two, count)
    low = exchange(from_one[:middle], two, count)
    high = exchange(from_two[middle:], one, count)
    pieces = [held, from_one, from_two, low, high]
    labels = [
        names,
        [name ^ one for name in names],
        [name ^ two for name in names],
        [name ^ one ^ two for name in names[:middle]],
        [name ^ one ^ two for name in names[middle:]],
    ]
    return pieces, labels


def body(tokens, norm_gain, caption, null_caption, keep, bucket_rows, w_qkv):
    grid_rows, grid_cols, features_count = tokens.shape[1:]
    token_count = grid_rows * grid_cols
    seq_size = lax.axis_size("seq")
    img_size = lax.axis_size("img")
    chips = seq_size // 2
    seq_at = lax.axis_index("seq")
    core = seq_at % 2
    swap = [(s, s ^ 1) for s in range(seq_size)]
    same_core = [[2 * z + c for z in range(chips)] for c in range(2)]
    depth = features_count // img_size
    padded = -(-depth // 16) * 16
    columns = w_qkv.shape[1] * seq_size
    inner = columns // 3
    half = inner // 2
    main = half // LANES * LANES
    rest = half - main

    gathered = lax.all_gather(w_qkv, "seq", axis=0)
    rows = jnp.transpose(gathered, (1, 0, 2)).reshape(depth, columns)
    rows = jnp.pad(rows, ((0, padded - depth), (0, 0)))

    def pick(part):
        low = rows[:, part * inner : part * inner + half]
        high = rows[:, part * inner + half : (part + 1) * inner]
        return jnp.where(core == 0, low, high)

    query_cols, key_cols, value_cols = pick(0), pick(1), pick(2)
    full = main // LANES
    split = main // 2
    first = jnp.concatenate(
        [key_cols, value_cols[:, main:], query_cols[:, :split]], axis=1
    )
    second = jnp.concatenate(
        [value_cols[:, :main], jnp.pad(query_cols[:, split:], ((0, 0), (0, LANES - rest)))],
        axis=1,
    )
    across, along = (1, 3), (4, 12)
    first_near, first_names = near_stage(first, across, img_size)
    second_near, second_names = near_stage(second, along, img_size)
    first_pieces, first_masks = far_stage(first_near, first_names, along, img_size)
    second_pieces, second_masks = far_stage(second_near, second_names, across, img_size)
    masks = (first_masks, second_masks)

    features = jnp.transpose(tokens[0], (0, 2, 1)).astype(jnp.float32)
    mean_square = jnp.mean(features * features, axis=1, keepdims=True)
    condition = jnp.where(keep[0] > 0, caption[0], null_caption).astype(jnp.float32)
    hidden = (
        features * lax.rsqrt(mean_square + norm_eps) * norm_gain.astype(jnp.float32)[None, :, None]
        + condition[None, :, None]
    ).astype(jnp.bfloat16)
    hidden = hidden.reshape(grid_rows, img_size, depth, grid_cols)
    hidden = jnp.pad(hidden, ((0, 0), (0, 0), (0, padded - depth), (0, 0)))
    order = jnp.bitwise_xor(lax.axis_index("img"), jnp.arange(img_size, dtype=jnp.int32))
    hidden = pl.pallas_call(
        reorder_kernel,
        in_specs=[SMEM, VMEM],
        out_specs=VMEM,
        out_shape=jax.ShapeDtypeStruct(hidden.shape, hidden.dtype),
        compiler_params=pltpu.CompilerParams(vmem_limit_bytes=8 * 1024 * 1024),
        name="reorder",
    )(order, hidden)
    hidden = hidden.reshape(grid_rows, img_size * padded, grid_cols)
    mine = jnp.transpose(hidden, (0, 2, 1)).reshape(token_count, img_size * padded)
    other = lax.ppermute(mine, "seq", swap)

    first_row = jnp.stack([seq_at, seq_at ^ 1]) * grid_rows
    live = jnp.clip(bucket_rows[0] - first_row, 0, grid_rows) * grid_cols

    part = compute_state(live, (mine, other), first_pieces, second_pieces, masks, full, chips)
    part = lax.all_to_all(part, "seq", 0, 0, axis_index_groups=same_core)
    queries = compute_queries((mine, other), first_pieces, second_pieces, masks, full)
    part = jnp.sum(part, axis=0)
    part = jnp.broadcast_to(part[None], (chips,) + part.shape)
    state = lax.all_to_all(part, "seq", 0, 0, axis_index_groups=same_core)

    own, far = compute_output(live, queries, state)
    back = lax.ppermute(far, "seq", swap)
    own, back = own[:, :half], back[:, :half]
    result = jnp.where(
        core == 0,
        jnp.concatenate([own, back], axis=1),
        jnp.concatenate([back, own], axis=1),
    )
    return result.reshape(1, grid_rows, grid_cols, inner)


def solution(mesh):
    in_specs = (
        P("img", "seq", None, None),
        P(),
        P("img", None),
        P(),
        P("img"),
        P("img"),
        P("img", "seq"),
    )
    out_specs = P("img", "seq", None, None)
    return jax.shard_map(body, mesh=mesh, in_specs=in_specs, out_specs=out_specs, check_vma=False)
```

```python
import jax
import jax.numpy as jnp
import numpy as np
from jax import lax
from jax.experimental import pallas as pl
from jax.experimental.pallas import tpu as pltpu
from jax.sharding import PartitionSpec as P


HDIM = 32
LANES = 128
GROUP = LANES // HDIM
TEAM = 4

norm_eps = 1e-06
attn_eps = 1e-06
HIGHEST = lax.Precision.HIGHEST

VMEM = pl.BlockSpec(memory_space=pltpu.VMEM)
SMEM = pl.BlockSpec(memory_space=pltpu.SMEM)
HBM = pl.BlockSpec(memory_space=pltpu.HBM)
PARAMS = pltpu.CompilerParams(vmem_limit_bytes=58 * 1024 * 1024)

FAR_MASKS = np.array([0] * 4 + [1] * 4 + [3] * 4 + [2] * 4)
NEAR_SLOTS = np.array([0, 1, 2, 3] * 3 + [0, 1] + [2, 3])


def block_mask():
    row = lax.broadcasted_iota(jnp.int32, (LANES, LANES), 0) // HDIM
    col = lax.broadcasted_iota(jnp.int32, (LANES, LANES), 1) // HDIM
    return row == col


def live_rows(limit, tokens):
    token = lax.broadcasted_iota(jnp.int32, (tokens, LANES), 0)
    return (token < limit).astype(jnp.float32)


def load_blocks(place_ref, base, pieces, start, into_ref, sems):
    depth, width = pieces[0].shape[1], into_ref.shape[1]
    copies = []
    for piece in pieces:
        for at in range(piece.shape[0]):
            count = len(copies)
            row = pl.multiple_of(place_ref[base + count] * depth, 16)
            copies.append(
                pltpu.make_async_copy(
                    piece.at[at, :, pl.ds(start, width)],
                    into_ref.at[pl.ds(row, depth), :],
                    sems.at[count],
                )
            )
    for copy in copies:
        copy.start()
    return copies


def load_hidden(hidden, into_ref, sems):
    copies = [
        pltpu.make_async_copy(ref, into_ref.at[at], sems.at[at])
        for at, ref in enumerate(hidden)
    ]
    for copy in copies:
        copy.start()
    return copies


def state_kernel(place_ref, live_ref, *refs):
    hidden, refs = refs[:TEAM], refs[TEAM:]
    first, second, refs = refs[:5], refs[5:10], refs[10:]
    out_ref, keys_ref, values_ref, pair_w, mixed_w, hidden_ref, pair_s, mixed_s, hidden_s = refs
    tokens = hidden_ref.shape[1]
    full = values_ref.shape[1] // LANES
    pair_copies = load_blocks(place_ref, 0, first, 0, pair_w, pair_s)
    hidden_copies = load_hidden(hidden, hidden_ref, hidden_s)
    mixed_copies = load_blocks(place_ref, 16, second, full * LANES, mixed_w, mixed_s)
    for copy in pair_copies:
        copy.wait()
    wide = full * LANES
    for at in range(TEAM):
        hidden_copies[at].wait()
        rows = slice(at * tokens, (at + 1) * tokens)
        block = hidden_ref[at]
        live = live_rows(live_ref[at], tokens)
        keys = jnp.dot(block, pair_w[:, :wide], preferred_element_type=jnp.float32)
        for tile in range(full):
            lanes = slice(tile * LANES, (tile + 1) * LANES)
            keys_ref[rows, lanes] = jnp.maximum(keys[:, lanes], 0.0) * live
        values_ref[rows, :] = jnp.dot(
            block, pair_w[:, wide:], preferred_element_type=jnp.float32
        )
        if at == 0:
            for copy in mixed_copies:
                copy.wait()
        keys_ref[rows, wide:] = jnp.dot(
            block, mixed_w[...], preferred_element_type=jnp.float32
        )
    same_head = block_mask()
    column = lax.broadcasted_iota(jnp.int32, (LANES, LANES), 1)
    chunks = out_ref.shape[0]
    rows = HDIM // chunks
    tiles = full + 1
    out_ref[...] = jnp.zeros_like(out_ref)
    for tile in range(tiles):
        keys = keys_ref[:, tile * LANES : (tile + 1) * LANES]
        if tile < full:
            values = values_ref[:, tile * LANES : (tile + 1) * LANES]
            keep = same_head
        else:
            values = pltpu.roll(keys, LANES - HDIM, 1)
            live = jnp.concatenate(
                [live_rows(live_ref[at], tokens) for at in range(TEAM)], axis=0
            )
            keys = jnp.maximum(keys, 0.0) * live
            keep = jnp.logical_and(same_head, column < HDIM)
        outer = lax.dot_general(
            keys,
            values,
            (((0,), (0,)), ((), ())),
            precision=HIGHEST,
            preferred_element_type=jnp.float32,
        )
        outer = jnp.where(keep, outer, 0.0)
        packed = outer[:HDIM]
        for head in range(1, GROUP):
            packed = packed + outer[head * HDIM : (head + 1) * HDIM]
        total = jnp.sum(keys, axis=0, keepdims=True)
        for chunk in range(chunks):
            for row in range(rows):
                source = chunk * rows + row
                target = row * tiles + tile
                out_ref[chunk, target : target + 1, :] = packed[source : source + 1]
            target = rows * tiles + tile
            out_ref[chunk, target : target + 1, :] = total


def query_kernel(place_ref, *refs):
    hidden, refs = refs[:TEAM], refs[TEAM:]
    second, refs = refs[:5], refs[5:]
    out_ref, weights_ref, hidden_ref, sems, hidden_s = refs
    tokens = hidden_ref.shape[1]
    copies = load_blocks(place_ref, 16, second, 0, weights_ref, sems)
    hidden_copies = load_hidden(hidden, hidden_ref, hidden_s)
    for copy in copies:
        copy.wait()
    for at in range(TEAM):
        hidden_copies[at].wait()
        rows = slice(at * tokens, (at + 1) * tokens)
        queries = jnp.dot(
            hidden_ref[at], weights_ref[...], preferred_element_type=jnp.float32
        )
        edge = out_ref.shape[1] - LANES
        out_ref[rows, :edge] = jnp.maximum(queries[:, :edge], 0.0)
        out_ref[rows, edge:] = jnp.maximum(
            pltpu.roll(queries[:, edge:], LANES - 2 * HDIM, 1), 0.0
        )


def attend_kernel(slot_ref, live_ref, query_ref, state_ref, out_ref):
    tokens = query_ref.shape[0]
    tiles = query_ref.shape[1] // LANES
    chunks = state_ref.shape[0]
    rows = HDIM // chunks
    live = live_rows(live_ref[pl.program_id(0)], tokens)
    same_head = block_mask()
    ones = same_head.astype(jnp.float32)
    for tile in range(tiles):
        query = query_ref[:, tile * LANES : (tile + 1) * LANES]
        packed = jnp.concatenate(
            [
                state_ref[chunk, row * tiles + tile : row * tiles + tile + 1, :]
                for chunk in range(chunks)
                for row in range(rows)
            ],
            axis=0,
        )
        state = jnp.where(same_head, jnp.concatenate([packed] * GROUP, axis=0), 0.0)
        total = state_ref[0, rows * tiles + tile : rows * tiles + tile + 1, :]
        numerator = jnp.dot(
            query, state, precision=HIGHEST, preferred_element_type=jnp.float32
        )
        denominator = jnp.dot(
            query * total, ones, precision=HIGHEST, preferred_element_type=jnp.float32
        )
        result = numerator / (denominator + attn_eps) * live
        out_ref[0, :, tile * LANES : (tile + 1) * LANES] = result.astype(jnp.bfloat16)


def compute_state(place, live, hidden, first, second, chunks):
    tokens, contraction = hidden[0].shape
    wide = first[0].shape[2] // 2
    tiles = wide // LANES + 1
    slots = -(-(HDIM // chunks + 1) * tiles // 8) * 8
    return pl.pallas_call(
        state_kernel,
        in_specs=[SMEM, SMEM] + [HBM] * (TEAM + len(first) + len(second)),
        out_specs=VMEM,
        out_shape=jax.ShapeDtypeStruct((chunks, slots, LANES), jnp.float32),
        scratch_shapes=[
            pltpu.VMEM((TEAM * tokens, wide + LANES), jnp.float32),
            pltpu.VMEM((TEAM * tokens, wide), jnp.float32),
            pltpu.VMEM((contraction, 2 * wide), jnp.bfloat16),
            pltpu.VMEM((contraction, LANES), jnp.bfloat16),
            pltpu.VMEM((TEAM, tokens, contraction), jnp.bfloat16),
            pltpu.SemaphoreType.DMA((16,)),
            pltpu.SemaphoreType.DMA((16,)),
            pltpu.SemaphoreType.DMA((TEAM,)),
        ],
        compiler_params=PARAMS,
        name="state",
    )(place, live, *hidden, *first, *second)


def compute_queries(place, hidden, second):
    tokens, contraction = hidden[0].shape
    width = second[0].shape[2]
    return pl.pallas_call(
        query_kernel,
        in_specs=[SMEM] + [HBM] * (TEAM + len(second)),
        out_specs=VMEM,
        out_shape=jax.ShapeDtypeStruct((TEAM * tokens, width), jnp.float32),
        scratch_shapes=[
            pltpu.VMEM((contraction, width), jnp.bfloat16),
            pltpu.VMEM((TEAM, tokens, contraction), jnp.bfloat16),
            pltpu.SemaphoreType.DMA((16,)),
            pltpu.SemaphoreType.DMA((TEAM,)),
        ],
        compiler_params=PARAMS,
        cost_estimate=pl.CostEstimate(
            flops=2 * TEAM * tokens * contraction * width,
            bytes_accessed=4 * TEAM * tokens * width + 2 * contraction * (width + TEAM * tokens),
            transcendentals=0,
        ),
        name="queries",
    )(place, *hidden, *second)


def compute_output(slots, live, queries, state):
    tokens, width = queries.shape[0] // TEAM, queries.shape[1]
    return pl.pallas_call(
        attend_kernel,
        grid_spec=pltpu.PrefetchScalarGridSpec(
            num_scalar_prefetch=2,
            grid=(TEAM,),
            in_specs=[
                pl.BlockSpec((tokens, width), lambda i, slots, live: (i, 0)),
                pl.BlockSpec(state.shape, lambda i, slots, live: (0, 0, 0)),
            ],
            out_specs=pl.BlockSpec((1, tokens, width), lambda i, slots, live: (slots[i], 0, 0)),
        ),
        out_shape=jax.ShapeDtypeStruct((TEAM, tokens, width), jnp.bfloat16),
        compiler_params=PARAMS,
        name="attend",
    )(slots, live, queries, state)


def spread(block, count, axis, groups):
    copies = jnp.broadcast_to(block[None], (count,) + block.shape)
    return lax.all_to_all(copies, axis, 0, 0, axis_index_groups=groups)


def exchange(block, mask, axis, count):
    return lax.ppermute(block, axis, [(i, i ^ mask) for i in range(count)])


def far_stage(held, one, two, count):
    middle = held.shape[0] // 2
    from_one = exchange(held, one, "img", count)
    from_two = exchange(held, two, "img", count)
    low = exchange(from_one[:middle], two, "img", count)
    high = exchange(from_two[middle:], one, "img", count)
    return [held, from_one, from_two, low, high]


def body(tokens, norm_gain, caption, null_caption, keep, bucket_rows, w_qkv):
    grid_rows, grid_cols, features_count = tokens.shape[1:]
    token_count = grid_rows * grid_cols
    seq_size = lax.axis_size("seq")
    img_size = lax.axis_size("img")
    side = 4
    teams = seq_size // TEAM
    seq_at = lax.axis_index("seq")
    img_at = lax.axis_index("img")
    rank = seq_at % TEAM
    same_rank = [[TEAM * j + r for j in range(teams)] for r in range(TEAM)]
    team = [[TEAM * j + r for r in range(TEAM)] for j in range(teams)]
    x_groups = [[y * side + x for x in range(side)] for y in range(side)]
    y_groups = [[y * side + x for y in range(side)] for x in range(side)]
    depth = features_count // img_size
    padded = -(-depth // 16) * 16
    columns = w_qkv.shape[1] * seq_size
    inner = columns // 3
    share = inner // TEAM
    main = share // LANES * LANES
    rest = share - main

    gathered = lax.all_gather(w_qkv, "seq", axis=0)
    rows = jnp.transpose(gathered, (1, 0, 2)).reshape(depth, columns)
    rows = jnp.pad(rows, ((0, padded - depth), (0, 0)))

    def pick(part):
        chosen = rows[:, part * inner : part * inner + share]
        for r in range(1, TEAM):
            start = part * inner + r * share
            chosen = jnp.where(rank == r, rows[:, start : start + share], chosen)
        return chosen

    query_cols, key_cols, value_cols = pick(0), pick(1), pick(2)
    first = jnp.concatenate([key_cols[:, :main], value_cols[:, :main]], axis=1)
    second = jnp.concatenate(
        [
            query_cols[:, :main],
            key_cols[:, main:],
            value_cols[:, main:],
            query_cols[:, main:],
            jnp.zeros((padded, LANES - 3 * rest), jnp.bfloat16),
        ],
        axis=1,
    )
    first_near = spread(first, side, "img", x_groups)
    second, tokens, first_near = lax.optimization_barrier((second, tokens, first_near))
    second_near = spread(second, side, "img", y_groups)
    first_pieces = far_stage(first_near, side, 3 * side, img_size)
    second_pieces = far_stage(second_near, 1, 3, img_size)
    y_at, x_at = img_at // side, img_at % side
    place = jnp.concatenate(
        [
            jnp.bitwise_xor(y_at, FAR_MASKS) * side + NEAR_SLOTS,
            NEAR_SLOTS * side + jnp.bitwise_xor(x_at, FAR_MASKS),
        ]
    ).astype(jnp.int32)

    features = jnp.transpose(tokens[0], (0, 2, 1)).astype(jnp.float32)
    mean_square = jnp.mean(features * features, axis=1, keepdims=True)
    condition = jnp.where(keep[0] > 0, caption[0], null_caption).astype(jnp.float32)
    hidden = (
        features * lax.rsqrt(mean_square + norm_eps) * norm_gain.astype(jnp.float32)[None, :, None]
        + condition[None, :, None]
    ).astype(jnp.bfloat16)
    hidden = hidden.reshape(grid_rows, img_size, depth, grid_cols)
    hidden = jnp.pad(hidden, ((0, 0), (0, 0), (0, padded - depth), (0, 0)))
    hidden = hidden.reshape(grid_rows, img_size * padded, grid_cols)
    mine = jnp.transpose(hidden, (0, 2, 1)).reshape(token_count, img_size * padded)
    beside = exchange(mine, 2, "seq", seq_size)
    late, _ = lax.optimization_barrier((beside, first_pieces[1:3] + second_pieces[1:3]))
    across = exchange(late, 1, "seq", seq_size)
    hidden = (mine, exchange(mine, 1, "seq", seq_size), beside, across)

    slots = jnp.bitwise_xor(rank, jnp.arange(TEAM, dtype=jnp.int32))
    first_row = (seq_at - rank + slots) * grid_rows
    live = jnp.clip(bucket_rows[0] - first_row, 0, grid_rows) * grid_cols

    part = compute_state(place, live, hidden, first_pieces, second_pieces, teams)
    part = lax.all_to_all(part, "seq", 0, 0, axis_index_groups=same_rank)
    state = spread(jnp.sum(part, axis=0), teams, "seq", same_rank)
    queries = compute_queries(place, hidden, second_pieces)

    result = compute_output(slots, live, queries, state)
    result = lax.all_to_all(result, "seq", 0, 0, axis_index_groups=team)
    result = jnp.transpose(result[:, :, :share], (1, 0, 2))
    return result.reshape(1, grid_rows, grid_cols, inner)


def solution(mesh):
    in_specs = (
        P("img", "seq", None, None),
        P(),
        P("img", None),
        P(),
        P("img"),
        P("img"),
        P("img", "seq"),
    )
    out_specs = P("img", "seq", None, None)

    return jax.shard_map(
        body, mesh=mesh, in_specs=in_specs, out_specs=out_specs, check_vma=False
    )
```

```python
import jax
import jax.numpy as jnp
import numpy as np
from jax import lax
from jax.experimental import pallas as pl
from jax.experimental.pallas import tpu as pltpu
from jax.sharding import PartitionSpec as P


HDIM = 32
LANES = 128
GROUP = LANES // HDIM
TEAM = 4

norm_eps = 1e-06
attn_eps = 1e-06

VMEM = pl.BlockSpec(memory_space=pltpu.VMEM)
SMEM = pl.BlockSpec(memory_space=pltpu.SMEM)
HBM = pl.BlockSpec(memory_space=pltpu.HBM)
PARAMS = pltpu.CompilerParams(vmem_limit_bytes=58 * 1024 * 1024)

FAR_MASKS = np.array([0] * 4 + [1] * 4 + [3] * 4 + [2] * 4)
NEAR_SLOTS = np.array([0, 1, 2, 3] * 3 + [0, 1] + [2, 3])


def block_mask():
    row = lax.broadcasted_iota(jnp.int32, (LANES, LANES), 0) // HDIM
    col = lax.broadcasted_iota(jnp.int32, (LANES, LANES), 1) // HDIM
    return row == col


def live_rows(limit, tokens):
    token = lax.broadcasted_iota(jnp.int32, (tokens, LANES), 0)
    return (token < limit).astype(jnp.float32)


def halves(value):
    high = value.astype(jnp.bfloat16)
    return high, (value - high.astype(jnp.float32)).astype(jnp.bfloat16)


def load_blocks(place_ref, base, pieces, start, into_ref, sems):
    depth, width = pieces[0].shape[1], into_ref.shape[1]
    copies = []
    for piece in pieces:
        for at in range(piece.shape[0]):
            count = len(copies)
            row = pl.multiple_of(place_ref[base + count] * depth, 16)
            copies.append(
                pltpu.make_async_copy(
                    piece.at[at, :, pl.ds(start, width)],
                    into_ref.at[pl.ds(row, depth), :],
                    sems.at[count],
                )
            )
    for copy in copies:
        copy.start()
    return copies


def load_hidden(hidden, into_ref, sems):
    copies = [
        pltpu.make_async_copy(ref, into_ref.at[at], sems.at[at])
        for at, ref in enumerate(hidden)
    ]
    for copy in copies:
        copy.start()
    return copies


def state_kernel(place_ref, live_ref, *refs):
    hidden, first, refs = refs[:TEAM], refs[TEAM : TEAM + 5], refs[TEAM + 5 :]
    out_ref, keys_ref, values_ref, weights_ref, hidden_ref, sems, hidden_s = refs
    tokens = hidden_ref.shape[1]
    full = values_ref.shape[1] // LANES
    copies = load_blocks(place_ref, 0, first, 0, weights_ref, sems)
    hidden_copies = load_hidden(hidden, hidden_ref, hidden_s)
    for copy in copies:
        copy.wait()
    wide = full * LANES
    for at in range(TEAM):
        hidden_copies[at].wait()
        rows = slice(at * tokens, (at + 1) * tokens)
        block = hidden_ref[at]
        live = live_rows(live_ref[at], tokens)
        keys = jnp.dot(block, weights_ref[:, :wide], preferred_element_type=jnp.float32)
        for tile in range(full):
            lanes = slice(tile * LANES, (tile + 1) * LANES)
            keys_ref[rows, lanes] = jnp.maximum(keys[:, lanes], 0.0) * live
        values_ref[rows, :] = jnp.dot(
            block, weights_ref[:, wide : 2 * wide], preferred_element_type=jnp.float32
        )
        keys_ref[rows, wide:] = jnp.dot(
            block, weights_ref[:, 2 * wide :], preferred_element_type=jnp.float32
        )
    same_head = block_mask()
    column = lax.broadcasted_iota(jnp.int32, (LANES, LANES), 1)
    chunks = out_ref.shape[0]
    rows = HDIM // chunks
    tiles = full + 1
    out_ref[...] = jnp.zeros_like(out_ref)
    for tile in range(tiles):
        keys = keys_ref[:, tile * LANES : (tile + 1) * LANES]
        if tile < full:
            values = values_ref[:, tile * LANES : (tile + 1) * LANES]
            keep = same_head
        else:
            values = pltpu.roll(keys, LANES - HDIM, 1)
            live = jnp.concatenate(
                [live_rows(live_ref[at], tokens) for at in range(TEAM)], axis=0
            )
            keys = jnp.maximum(keys, 0.0) * live
            keep = jnp.logical_and(same_head, column < HDIM)
        key_high, key_low = halves(keys)
        value_high, value_low = halves(values)
        tall = (((0,), (0,)), ((), ()))
        both = lax.dot_general(
            key_high,
            jnp.concatenate([value_high, value_low], axis=1),
            tall,
            preferred_element_type=jnp.float32,
        )
        outer = lax.dot_general(key_low, value_high, tall, preferred_element_type=jnp.float32)
        outer = outer + both[:, LANES:] + both[:, :LANES]
        outer = jnp.where(keep, outer, 0.0)
        packed = outer[:HDIM]
        for head in range(1, GROUP):
            packed = packed + outer[head * HDIM : (head + 1) * HDIM]
        total = jnp.sum(keys, axis=0, keepdims=True)
        for chunk in range(chunks):
            for row in range(rows):
                source = chunk * rows + row
                target = row * tiles + tile
                out_ref[chunk, target : target + 1, :] = packed[source : source + 1]
            target = rows * tiles + tile
            out_ref[chunk, target : target + 1, :] = total


def query_kernel(place_ref, *refs):
    hidden, refs = refs[:TEAM], refs[TEAM:]
    second, refs = refs[:5], refs[5:]
    out_ref, weights_ref, hidden_ref, sems, hidden_s = refs
    tokens = hidden_ref.shape[1]
    copies = load_blocks(place_ref, 16, second, 0, weights_ref, sems)
    hidden_copies = load_hidden(hidden, hidden_ref, hidden_s)
    for copy in copies:
        copy.wait()
    for at in range(TEAM):
        hidden_copies[at].wait()
        rows = slice(at * tokens, (at + 1) * tokens)
        queries = jnp.dot(
            hidden_ref[at], weights_ref[...], preferred_element_type=jnp.float32
        )
        out_ref[rows, :] = jnp.maximum(queries, 0.0)


def attend_kernel(slot_ref, live_ref, query_ref, state_ref, out_ref, factor_ref):
    tokens = query_ref.shape[0]
    tiles = query_ref.shape[1] // LANES
    chunks = state_ref.shape[0]
    rows = HDIM // chunks

    @pl.when(pl.program_id(0) == 0)
    def _():
        same_head = block_mask()
        for tile in range(tiles):
            packed = jnp.concatenate(
                [
                    state_ref[chunk, row * tiles + tile : row * tiles + tile + 1, :]
                    for chunk in range(chunks)
                    for row in range(rows)
                ],
                axis=0,
            )
            state = jnp.where(same_head, jnp.concatenate([packed] * GROUP, axis=0), 0.0)
            total = state_ref[0, rows * tiles + tile : rows * tiles + tile + 1, :]
            total = jnp.transpose(jnp.broadcast_to(total, (LANES, LANES)))
            total = jnp.where(same_head, total, 0.0)
            high, low = halves(jnp.concatenate([state, total], axis=1))
            factor_ref[tile, :, : 2 * LANES] = high
            factor_ref[tile, :, 2 * LANES :] = low

    live = live_rows(live_ref[pl.program_id(0)], tokens)
    for tile in range(tiles):
        high, low = halves(query_ref[:, tile * LANES : (tile + 1) * LANES])
        main = jnp.dot(high, factor_ref[tile], preferred_element_type=jnp.float32)
        small = jnp.dot(
            low, factor_ref[tile, :, : 2 * LANES], preferred_element_type=jnp.float32
        )
        total = main[:, 2 * LANES :] + small + main[:, : 2 * LANES]
        result = total[:, :LANES] / (total[:, LANES:] + attn_eps) * live
        out_ref[0, :, tile * LANES : (tile + 1) * LANES] = result.astype(jnp.bfloat16)


def compute_state(place, live, hidden, first, chunks):
    tokens, contraction = hidden[0].shape
    wide = (first[0].shape[2] - LANES) // 2
    tiles = wide // LANES + 1
    slots = -(-(HDIM // chunks + 1) * tiles // 8) * 8
    return pl.pallas_call(
        state_kernel,
        in_specs=[SMEM, SMEM] + [HBM] * (TEAM + len(first)),
        out_specs=VMEM,
        out_shape=jax.ShapeDtypeStruct((chunks, slots, LANES), jnp.float32),
        scratch_shapes=[
            pltpu.VMEM((TEAM * tokens, wide + LANES), jnp.float32),
            pltpu.VMEM((TEAM * tokens, wide), jnp.float32),
            pltpu.VMEM((contraction, 2 * wide + LANES), jnp.bfloat16),
            pltpu.VMEM((TEAM, tokens, contraction), jnp.bfloat16),
            pltpu.SemaphoreType.DMA((16,)),
            pltpu.SemaphoreType.DMA((TEAM,)),
        ],
        compiler_params=PARAMS,
        name="state",
    )(place, live, *hidden, *first)


def compute_queries(place, hidden, second):
    tokens, contraction = hidden[0].shape
    width = second[0].shape[2]
    return pl.pallas_call(
        query_kernel,
        in_specs=[SMEM] + [HBM] * (TEAM + len(second)),
        out_specs=VMEM,
        out_shape=jax.ShapeDtypeStruct((TEAM * tokens, width), jnp.float32),
        scratch_shapes=[
            pltpu.VMEM((contraction, width), jnp.bfloat16),
            pltpu.VMEM((TEAM, tokens, contraction), jnp.bfloat16),
            pltpu.SemaphoreType.DMA((16,)),
            pltpu.SemaphoreType.DMA((TEAM,)),
        ],
        compiler_params=PARAMS,
        cost_estimate=pl.CostEstimate(
            flops=2 * TEAM * tokens * contraction * width,
            bytes_accessed=4 * TEAM * tokens * width + 2 * contraction * (width + TEAM * tokens),
            transcendentals=0,
        ),
        name="queries",
    )(place, *hidden, *second)


def compute_output(slots, live, queries, state):
    tokens, width = queries.shape[0] // TEAM, queries.shape[1]
    return pl.pallas_call(
        attend_kernel,
        grid_spec=pltpu.PrefetchScalarGridSpec(
            num_scalar_prefetch=2,
            grid=(TEAM,),
            in_specs=[
                pl.BlockSpec((tokens, width), lambda i, slots, live: (i, 0)),
                pl.BlockSpec(state.shape, lambda i, slots, live: (0, 0, 0)),
            ],
            out_specs=pl.BlockSpec((1, tokens, width), lambda i, slots, live: (slots[i], 0, 0)),
            scratch_shapes=[pltpu.VMEM((width // LANES, LANES, 4 * LANES), jnp.bfloat16)],
        ),
        out_shape=jax.ShapeDtypeStruct((TEAM, tokens, width), jnp.bfloat16),
        compiler_params=PARAMS,
        name="attend",
    )(slots, live, queries, state)


def spread(block, count, axis, groups):
    copies = jnp.broadcast_to(block[None], (count,) + block.shape)
    return lax.all_to_all(copies, axis, 0, 0, axis_index_groups=groups)


def exchange(block, mask, axis, count):
    return lax.ppermute(block, axis, [(i, i ^ mask) for i in range(count)])


def far_stage(held, one, two, count):
    middle = held.shape[0] // 2
    from_one = exchange(held, one, "img", count)
    from_two = exchange(held, two, "img", count)
    low = exchange(from_one[:middle], two, "img", count)
    high = exchange(from_two[middle:], one, "img", count)
    return [held, from_one, from_two, low, high]


def body(tokens, norm_gain, caption, null_caption, keep, bucket_rows, w_qkv):
    grid_rows, grid_cols, features_count = tokens.shape[1:]
    token_count = grid_rows * grid_cols
    seq_size = lax.axis_size("seq")
    img_size = lax.axis_size("img")
    side = 4
    teams = seq_size // TEAM
    seq_at = lax.axis_index("seq")
    img_at = lax.axis_index("img")
    rank = seq_at % TEAM
    same_rank = [[TEAM * j + r for j in range(teams)] for r in range(TEAM)]
    team = [[TEAM * j + r for r in range(TEAM)] for j in range(teams)]
    x_groups = [[y * side + x for x in range(side)] for y in range(side)]
    y_groups = [[y * side + x for y in range(side)] for x in range(side)]
    depth = features_count // img_size
    padded = -(-depth // 16) * 16
    columns = w_qkv.shape[1] * seq_size
    inner = columns // 3
    share = inner // TEAM
    main = share // LANES * LANES
    rest = share - main

    gathered = lax.all_gather(w_qkv, "seq", axis=0)
    rows = jnp.transpose(gathered, (1, 0, 2)).reshape(depth, columns)
    rows = jnp.pad(rows, ((0, padded - depth), (0, 0)))

    def pick(part):
        chosen = rows[:, part * inner : part * inner + share]
        for r in range(1, TEAM):
            start = part * inner + r * share
            chosen = jnp.where(rank == r, rows[:, start : start + share], chosen)
        return chosen

    query_cols, key_cols, value_cols = pick(0), pick(1), pick(2)
    first = jnp.concatenate(
        [
            key_cols[:, :main],
            value_cols[:, :main],
            key_cols[:, main:],
            value_cols[:, main:],
            jnp.zeros((padded, LANES - 2 * rest), jnp.bfloat16),
        ],
        axis=1,
    )
    second = jnp.pad(query_cols, ((0, 0), (0, LANES - rest)))
    first, tokens = lax.optimization_barrier((first, tokens))
    first_near = spread(first, side, "img", x_groups)
    second, first_near = lax.optimization_barrier((second, first_near))
    second_near = spread(second, side, "img", y_groups)
    first_pieces = far_stage(first_near, side, 3 * side, img_size)
    second_pieces = far_stage(second_near, 1, 3, img_size)
    y_at, x_at = img_at // side, img_at % side
    place = jnp.concatenate(
        [
            jnp.bitwise_xor(y_at, FAR_MASKS) * side + NEAR_SLOTS,
            NEAR_SLOTS * side + jnp.bitwise_xor(x_at, FAR_MASKS),
        ]
    ).astype(jnp.int32)

    features = jnp.transpose(tokens[0], (0, 2, 1)).astype(jnp.float32)
    mean_square = jnp.mean(features * features, axis=1, keepdims=True)
    condition = jnp.where(keep[0] > 0, caption[0], null_caption).astype(jnp.float32)
    hidden = (
        features * lax.rsqrt(mean_square + norm_eps) * norm_gain.astype(jnp.float32)[None, :, None]
        + condition[None, :, None]
    ).astype(jnp.bfloat16)
    hidden = hidden.reshape(grid_rows, img_size, depth, grid_cols)
    hidden = jnp.pad(hidden, ((0, 0), (0, 0), (0, padded - depth), (0, 0)))
    hidden = hidden.reshape(grid_rows, img_size * padded, grid_cols)
    mine = jnp.transpose(hidden, (0, 2, 1)).reshape(token_count, img_size * padded)
    beside = exchange(mine, 2, "seq", seq_size)
    late, _ = lax.optimization_barrier((beside, first_pieces[1:3]))
    across = exchange(late, 1, "seq", seq_size)
    hidden = (mine, exchange(mine, 1, "seq", seq_size), beside, across)

    slots = jnp.bitwise_xor(rank, jnp.arange(TEAM, dtype=jnp.int32))
    first_row = (seq_at - rank + slots) * grid_rows
    live = jnp.clip(bucket_rows[0] - first_row, 0, grid_rows) * grid_cols

    part = compute_state(place, live, hidden, first_pieces, teams)
    part = lax.all_to_all(part, "seq", 0, 0, axis_index_groups=same_rank)
    state = spread(jnp.sum(part, axis=0), teams, "seq", same_rank)
    queries = compute_queries(place, hidden, second_pieces)

    result = compute_output(slots, live, queries, state)
    result = lax.all_to_all(result, "seq", 0, 0, axis_index_groups=team)
    result = jnp.transpose(result[:, :, :share], (1, 0, 2))
    return result.reshape(1, grid_rows, grid_cols, inner)


def solution(mesh):
    in_specs = (
        P("img", "seq", None, None),
        P(),
        P("img", None),
        P(),
        P("img"),
        P("img"),
        P("img", "seq"),
    )
    out_specs = P("img", "seq", None, None)

    return jax.shard_map(
        body, mesh=mesh, in_specs=in_specs, out_specs=out_specs, check_vma=False
    )
```

```python
import jax
import jax.numpy as jnp
import numpy as np
from jax import lax
from jax.experimental import pallas as pl
from jax.experimental.pallas import tpu as pltpu
from jax.sharding import PartitionSpec as P


HDIM = 32
LANES = 128
GROUP = LANES // HDIM
TEAM = 4

norm_eps = 1e-06
attn_eps = 1e-06

VMEM = pl.BlockSpec(memory_space=pltpu.VMEM)
SMEM = pl.BlockSpec(memory_space=pltpu.SMEM)
HBM = pl.BlockSpec(memory_space=pltpu.HBM)
PARAMS = pltpu.CompilerParams(vmem_limit_bytes=58 * 1024 * 1024)

FAR_MASKS = np.array([0] * 4 + [1] * 4 + [3] * 4 + [2] * 4)
NEAR_SLOTS = np.array([0, 1, 2, 3] * 4)
PIECES = 4


def block_mask():
    row = lax.broadcasted_iota(jnp.int32, (LANES, LANES), 0) // HDIM
    col = lax.broadcasted_iota(jnp.int32, (LANES, LANES), 1) // HDIM
    return row == col


def live_rows(limit, tokens):
    token = lax.broadcasted_iota(jnp.int32, (tokens, LANES), 0)
    return (token < limit).astype(jnp.float32)


def halves(value):
    high = value.astype(jnp.bfloat16)
    return high, (value - high.astype(jnp.float32)).astype(jnp.bfloat16)


def load_blocks(place_ref, base, pieces, start, into_ref, sems):
    depth, width = pieces[0].shape[1], into_ref.shape[1]
    copies = []
    for piece in pieces:
        for at in range(piece.shape[0]):
            count = len(copies)
            row = pl.multiple_of(place_ref[base + count] * depth, 16)
            copies.append(
                pltpu.make_async_copy(
                    piece.at[at, :, pl.ds(start, width)],
                    into_ref.at[pl.ds(row, depth), :],
                    sems.at[count],
                )
            )
    for copy in copies:
        copy.start()
    return copies


def load_hidden(hidden, into_ref, sems):
    copies = [
        pltpu.make_async_copy(ref, into_ref.at[at], sems.at[at])
        for at, ref in enumerate(hidden)
    ]
    for copy in copies:
        copy.start()
    return copies


def state_kernel(place_ref, live_ref, *refs):
    hidden, first, refs = refs[:TEAM], refs[TEAM : TEAM + PIECES], refs[TEAM + PIECES :]
    out_ref, keys_ref, values_ref, weights_ref, hidden_ref, sems, hidden_s = refs
    tokens = hidden_ref.shape[1]
    full = values_ref.shape[1] // LANES
    copies = load_blocks(place_ref, 0, first, 0, weights_ref, sems)
    hidden_copies = load_hidden(hidden, hidden_ref, hidden_s)
    for copy in copies:
        copy.wait()
    wide = full * LANES
    for at in range(TEAM):
        hidden_copies[at].wait()
        rows = slice(at * tokens, (at + 1) * tokens)
        block = hidden_ref[at]
        live = live_rows(live_ref[at], tokens)
        keys = jnp.dot(block, weights_ref[:, :wide], preferred_element_type=jnp.float32)
        for tile in range(full):
            lanes = slice(tile * LANES, (tile + 1) * LANES)
            keys_ref[rows, lanes] = jnp.maximum(keys[:, lanes], 0.0) * live
        values_ref[rows, :] = jnp.dot(
            block, weights_ref[:, wide : 2 * wide], preferred_element_type=jnp.float32
        )
        keys_ref[rows, wide:] = jnp.dot(
            block, weights_ref[:, 2 * wide :], preferred_element_type=jnp.float32
        )
    same_head = block_mask()
    column = lax.broadcasted_iota(jnp.int32, (LANES, LANES), 1)
    tiles = full + 1
    tail = full * HDIM
    fold = HDIM // GROUP
    out_ref[...] = jnp.zeros_like(out_ref)
    for tile in range(tiles):
        keys = keys_ref[:, tile * LANES : (tile + 1) * LANES]
        if tile < full:
            values = values_ref[:, tile * LANES : (tile + 1) * LANES]
            keep = same_head
        else:
            values = pltpu.roll(keys, LANES - HDIM, 1)
            live = jnp.concatenate(
                [live_rows(live_ref[at], tokens) for at in range(TEAM)], axis=0
            )
            keys = jnp.maximum(keys, 0.0) * live
            keep = jnp.logical_and(same_head, column < HDIM)
        key_high, key_low = halves(keys)
        value_high, value_low = halves(values)
        tall = (((0,), (0,)), ((), ()))
        both = lax.dot_general(
            key_high,
            jnp.concatenate([value_high, value_low], axis=1),
            tall,
            preferred_element_type=jnp.float32,
        )
        outer = lax.dot_general(key_low, value_high, tall, preferred_element_type=jnp.float32)
        outer = outer + both[:, LANES:] + both[:, :LANES]
        outer = jnp.where(keep, outer, 0.0)
        packed = outer[:HDIM]
        for head in range(1, GROUP):
            packed = packed + outer[head * HDIM : (head + 1) * HDIM]
        if tile < full:
            out_ref[tile * HDIM : (tile + 1) * HDIM, :] = packed
        else:
            folded = packed[:fold]
            for part in range(1, GROUP):
                folded = folded + pltpu.roll(
                    packed[part * fold : (part + 1) * fold], part * HDIM, 1
                )
            out_ref[tail : tail + fold, :] = folded
        out_ref[tail + fold + tile : tail + fold + tile + 1, :] = jnp.sum(
            keys, axis=0, keepdims=True
        )


def query_kernel(place_ref, *refs):
    hidden, refs = refs[:TEAM], refs[TEAM:]
    second, refs = refs[:PIECES], refs[PIECES:]
    out_ref, weights_ref, hidden_ref, sems, hidden_s = refs
    tokens = hidden_ref.shape[1]
    copies = load_blocks(place_ref, 16, second, 0, weights_ref, sems)
    hidden_copies = load_hidden(hidden, hidden_ref, hidden_s)
    for copy in copies:
        copy.wait()
    for at in range(TEAM):
        hidden_copies[at].wait()
        rows = slice(at * tokens, (at + 1) * tokens)
        queries = jnp.dot(
            hidden_ref[at], weights_ref[...], preferred_element_type=jnp.float32
        )
        out_ref[rows, :] = jnp.maximum(queries, 0.0)


def attend_kernel(slot_ref, live_ref, query_ref, state_ref, out_ref, factor_ref):
    tokens = query_ref.shape[0]
    tiles = query_ref.shape[1] // LANES
    tail = (tiles - 1) * HDIM
    fold = HDIM // GROUP

    @pl.when(pl.program_id(0) == 0)
    def _():
        same_head = block_mask()
        summed = jnp.sum(state_ref[...], axis=0)
        for tile in range(tiles):
            if tile < tiles - 1:
                packed = summed[tile * HDIM : (tile + 1) * HDIM]
            else:
                folded = summed[tail : tail + fold]
                packed = jnp.concatenate(
                    [folded]
                    + [pltpu.roll(folded, LANES - part * HDIM, 1) for part in range(1, GROUP)],
                    axis=0,
                )
            state = jnp.where(same_head, jnp.concatenate([packed] * GROUP, axis=0), 0.0)
            total = summed[tail + fold + tile : tail + fold + tile + 1]
            total = jnp.transpose(jnp.broadcast_to(total, (LANES, LANES)))
            total = jnp.where(same_head, total, 0.0)
            high, low = halves(jnp.concatenate([state, total], axis=1))
            factor_ref[tile, :, : 2 * LANES] = high
            factor_ref[tile, :, 2 * LANES :] = low

    live = live_rows(live_ref[pl.program_id(0)], tokens)
    for tile in range(tiles):
        high, low = halves(query_ref[:, tile * LANES : (tile + 1) * LANES])
        main = jnp.dot(high, factor_ref[tile], preferred_element_type=jnp.float32)
        small = jnp.dot(
            low, factor_ref[tile, :, : 2 * LANES], preferred_element_type=jnp.float32
        )
        total = main[:, 2 * LANES :] + small + main[:, : 2 * LANES]
        result = total[:, :LANES] / (total[:, LANES:] + attn_eps) * live
        out_ref[0, :, tile * LANES : (tile + 1) * LANES] = result.astype(jnp.bfloat16)


def compute_state(place, live, hidden, first):
    tokens, contraction = hidden[0].shape
    wide = (first[0].shape[2] - LANES) // 2
    tiles = wide // LANES + 1
    slots = -(-((tiles - 1) * HDIM + HDIM // GROUP + tiles) // 8) * 8
    return pl.pallas_call(
        state_kernel,
        in_specs=[SMEM, SMEM] + [HBM] * (TEAM + len(first)),
        out_specs=VMEM,
        out_shape=jax.ShapeDtypeStruct((slots, LANES), jnp.float32),
        scratch_shapes=[
            pltpu.VMEM((TEAM * tokens, wide + LANES), jnp.float32),
            pltpu.VMEM((TEAM * tokens, wide), jnp.float32),
            pltpu.VMEM((contraction, 2 * wide + LANES), jnp.bfloat16),
            pltpu.VMEM((TEAM, tokens, contraction), jnp.bfloat16),
            pltpu.SemaphoreType.DMA((16,)),
            pltpu.SemaphoreType.DMA((TEAM,)),
        ],
        compiler_params=PARAMS,
        name="state",
    )(place, live, *hidden, *first)


def compute_queries(place, hidden, second):
    tokens, contraction = hidden[0].shape
    width = second[0].shape[2]
    return pl.pallas_call(
        query_kernel,
        in_specs=[SMEM] + [HBM] * (TEAM + len(second)),
        out_specs=VMEM,
        out_shape=jax.ShapeDtypeStruct((TEAM * tokens, width), jnp.float32),
        scratch_shapes=[
            pltpu.VMEM((contraction, width), jnp.bfloat16),
            pltpu.VMEM((TEAM, tokens, contraction), jnp.bfloat16),
            pltpu.SemaphoreType.DMA((16,)),
            pltpu.SemaphoreType.DMA((TEAM,)),
        ],
        compiler_params=PARAMS,
        cost_estimate=pl.CostEstimate(
            flops=2 * TEAM * tokens * contraction * width,
            bytes_accessed=4 * TEAM * tokens * width + 2 * contraction * (width + TEAM * tokens),
            transcendentals=0,
        ),
        name="queries",
    )(place, *hidden, *second)


def compute_output(slots, live, queries, state):
    tokens, width = queries.shape[0] // TEAM, queries.shape[1]
    return pl.pallas_call(
        attend_kernel,
        grid_spec=pltpu.PrefetchScalarGridSpec(
            num_scalar_prefetch=2,
            grid=(TEAM,),
            in_specs=[
                pl.BlockSpec((tokens, width), lambda i, slots, live: (i, 0)),
                pl.BlockSpec(state.shape, lambda i, slots, live: (0, 0, 0)),
            ],
            out_specs=pl.BlockSpec((1, tokens, width), lambda i, slots, live: (slots[i], 0, 0)),
            scratch_shapes=[pltpu.VMEM((width // LANES, LANES, 4 * LANES), jnp.bfloat16)],
        ),
        out_shape=jax.ShapeDtypeStruct((TEAM, tokens, width), jnp.bfloat16),
        compiler_params=PARAMS,
        name="attend",
    )(slots, live, queries, state)


def spread(block, count, axis, groups):
    copies = jnp.broadcast_to(block[None], (count,) + block.shape)
    return lax.all_to_all(copies, axis, 0, 0, axis_index_groups=groups)


def exchange(block, mask, axis, count):
    return lax.ppermute(block, axis, [(i, i ^ mask) for i in range(count)])


def far_stage(held, one, two, count):
    from_one = exchange(held, one, "img", count)
    from_two = exchange(held, two, "img", count)
    opposite = exchange(from_one, two, "img", count)
    return [held, from_one, from_two, opposite]


def body(tokens, norm_gain, caption, null_caption, keep, bucket_rows, w_qkv):
    grid_rows, grid_cols, features_count = tokens.shape[1:]
    token_count = grid_rows * grid_cols
    seq_size = lax.axis_size("seq")
    img_size = lax.axis_size("img")
    side = 4
    teams = seq_size // TEAM
    seq_at = lax.axis_index("seq")
    img_at = lax.axis_index("img")
    rank = seq_at % TEAM
    same_rank = [[TEAM * j + r for j in range(teams)] for r in range(TEAM)]
    team = [[TEAM * j + r for r in range(TEAM)] for j in range(teams)]
    x_groups = [[y * side + x for x in range(side)] for y in range(side)]
    y_groups = [[y * side + x for y in range(side)] for x in range(side)]
    depth = features_count // img_size
    padded = -(-depth // 16) * 16
    columns = w_qkv.shape[1] * seq_size
    inner = columns // 3
    share = inner // TEAM
    main = share // LANES * LANES
    rest = share - main

    gathered = lax.all_gather(w_qkv, "seq", axis=0)
    rows = jnp.transpose(gathered, (1, 0, 2)).reshape(depth, columns)
    rows = jnp.pad(rows, ((0, padded - depth), (0, 0)))

    def pick(part):
        chosen = rows[:, part * inner : part * inner + share]
        for r in range(1, TEAM):
            start = part * inner + r * share
            chosen = jnp.where(rank == r, rows[:, start : start + share], chosen)
        return chosen

    query_cols, key_cols, value_cols = pick(0), pick(1), pick(2)
    first = jnp.concatenate(
        [
            key_cols[:, :main],
            value_cols[:, :main],
            key_cols[:, main:],
            value_cols[:, main:],
            jnp.zeros((padded, LANES - 2 * rest), jnp.bfloat16),
        ],
        axis=1,
    )
    second = jnp.pad(query_cols, ((0, 0), (0, LANES - rest)))
    first, tokens = lax.optimization_barrier((first, tokens))
    first_near = spread(first, side, "img", x_groups)
    y_at, x_at = img_at // side, img_at % side
    place = jnp.concatenate(
        [
            jnp.bitwise_xor(y_at, FAR_MASKS) * side + NEAR_SLOTS,
            NEAR_SLOTS * side + jnp.bitwise_xor(x_at, FAR_MASKS),
        ]
    ).astype(jnp.int32)
    slots = jnp.bitwise_xor(rank, jnp.arange(TEAM, dtype=jnp.int32))
    first_row = (seq_at - rank + slots) * grid_rows
    live = jnp.clip(bucket_rows[0] - first_row, 0, grid_rows) * grid_cols
    second, first_near, place, live, slots = lax.optimization_barrier(
        (second, first_near, place, live, slots)
    )
    second_near = spread(second, side, "img", y_groups)
    first_pieces = far_stage(first_near, side, 3 * side, img_size)
    second_pieces = far_stage(second_near, 1, 3, img_size)
    features = jnp.transpose(tokens[0], (0, 2, 1)).astype(jnp.float32)
    mean_square = jnp.mean(features * features, axis=1, keepdims=True)
    condition = jnp.where(keep[0] > 0, caption[0], null_caption).astype(jnp.float32)
    hidden = (
        features * lax.rsqrt(mean_square + norm_eps) * norm_gain.astype(jnp.float32)[None, :, None]
        + condition[None, :, None]
    ).astype(jnp.bfloat16)
    hidden = hidden.reshape(grid_rows, img_size, depth, grid_cols)
    hidden = jnp.pad(hidden, ((0, 0), (0, 0), (0, padded - depth), (0, 0)))
    hidden = hidden.reshape(grid_rows, img_size * padded, grid_cols)
    mine = jnp.transpose(hidden, (0, 2, 1)).reshape(token_count, img_size * padded)
    beside = exchange(mine, 2, "seq", seq_size)
    late, _ = lax.optimization_barrier((beside, first_pieces[1:3]))
    across = exchange(late, 1, "seq", seq_size)
    hidden = (mine, exchange(mine, 1, "seq", seq_size), beside, across)

    part = compute_state(place, live, hidden, first_pieces)
    state = spread(part, teams, "seq", same_rank)
    queries = compute_queries(place, hidden, second_pieces)

    result = compute_output(slots, live, queries, state)
    result = lax.all_to_all(result, "seq", 0, 0, axis_index_groups=team)
    result = jnp.transpose(result[:, :, :share], (1, 0, 2))
    return result.reshape(1, grid_rows, grid_cols, inner)


def solution(mesh):
    in_specs = (
        P("img", "seq", None, None),
        P(),
        P("img", None),
        P(),
        P("img"),
        P("img"),
        P("img", "seq"),
    )
    out_specs = P("img", "seq", None, None)

    return jax.shard_map(
        body, mesh=mesh, in_specs=in_specs, out_specs=out_specs, check_vma=False
    )
```

```python
import jax
import jax.numpy as jnp
import numpy as np
from jax import lax
from jax.experimental import pallas as pl
from jax.experimental.pallas import tpu as pltpu
from jax.sharding import PartitionSpec as P


HDIM = 32
LANES = 128
GROUP = LANES // HDIM
TEAM = 4

norm_eps = 1e-06
attn_eps = 1e-06

VMEM = pl.BlockSpec(memory_space=pltpu.VMEM)
SMEM = pl.BlockSpec(memory_space=pltpu.SMEM)
HBM = pl.BlockSpec(memory_space=pl.ANY)
PARAMS = pltpu.CompilerParams(vmem_limit_bytes=32 * 1024 * 1024)

FAR_MASKS = np.array([0] * 4 + [1] * 4 + [3] * 4 + [2] * 4)
NEAR_SLOTS = np.array([0, 1, 2, 3] * 4)
PIECES = 4


def block_mask():
    row = lax.broadcasted_iota(jnp.int32, (LANES, LANES), 0) // HDIM
    col = lax.broadcasted_iota(jnp.int32, (LANES, LANES), 1) // HDIM
    return row == col


def live_rows(limit, tokens):
    token = lax.broadcasted_iota(jnp.int32, (tokens, LANES), 0)
    return (token < limit).astype(jnp.float32)


def halves(value):
    high = value.astype(jnp.bfloat16)
    return high, (value - high.astype(jnp.float32)).astype(jnp.bfloat16)


def load_blocks(place_ref, base, pieces, start, into_ref, sems):
    depth, width = pieces[0].shape[1], into_ref.shape[1]
    copies = []
    for piece in pieces:
        for at in range(piece.shape[0]):
            count = len(copies)
            row = pl.multiple_of(place_ref[base + count] * depth, 16)
            copies.append(
                pltpu.make_async_copy(
                    piece.at[at, :, pl.ds(start, width)],
                    into_ref.at[pl.ds(row, depth), :],
                    sems.at[count],
                )
            )
    for copy in copies:
        copy.start()
    return copies


def load_hidden(hidden, into_ref, sems):
    copies = [
        pltpu.make_async_copy(ref, into_ref.at[at], sems.at[at])
        for at, ref in enumerate(hidden)
    ]
    for copy in copies:
        copy.start()
    return copies


def state_kernel(place_ref, live_ref, *refs):
    hidden, first, refs = refs[:TEAM], refs[TEAM : TEAM + PIECES], refs[TEAM + PIECES :]
    out_ref, keys_ref, values_ref, weights_ref, hidden_ref, sems, hidden_s = refs
    tokens = hidden_ref.shape[1]
    full = values_ref.shape[1] // LANES
    copies = load_blocks(place_ref, 0, first, 0, weights_ref, sems)
    hidden_copies = load_hidden(hidden, hidden_ref, hidden_s)
    for copy in copies:
        copy.wait()
    wide = full * LANES
    for at in range(TEAM):
        hidden_copies[at].wait()
        rows = slice(at * tokens, (at + 1) * tokens)
        block = hidden_ref[at]
        live = live_rows(live_ref[at], tokens)
        keys = jnp.dot(block, weights_ref[:, :wide], preferred_element_type=jnp.float32)
        for tile in range(full):
            lanes = slice(tile * LANES, (tile + 1) * LANES)
            keys_ref[rows, lanes] = jnp.maximum(keys[:, lanes], 0.0) * live
        values_ref[rows, :] = jnp.dot(
            block, weights_ref[:, wide : 2 * wide], preferred_element_type=jnp.float32
        )
        keys_ref[rows, wide:] = jnp.dot(
            block, weights_ref[:, 2 * wide :], preferred_element_type=jnp.float32
        )
    same_head = block_mask()
    column = lax.broadcasted_iota(jnp.int32, (LANES, LANES), 1)
    tiles = full + 1
    tail = full * HDIM
    fold = HDIM // GROUP
    out_ref[...] = jnp.zeros_like(out_ref)
    for tile in range(tiles):
        keys = keys_ref[:, tile * LANES : (tile + 1) * LANES]
        if tile < full:
            values = values_ref[:, tile * LANES : (tile + 1) * LANES]
            keep = same_head
        else:
            values = pltpu.roll(keys, LANES - HDIM, 1)
            live = jnp.concatenate(
                [live_rows(live_ref[at], tokens) for at in range(TEAM)], axis=0
            )
            keys = jnp.maximum(keys, 0.0) * live
            keep = jnp.logical_and(same_head, column < HDIM)
        key_high, key_low = halves(keys)
        value_high, value_low = halves(values)
        tall = (((0,), (0,)), ((), ()))
        both = lax.dot_general(
            key_high,
            jnp.concatenate([value_high, value_low], axis=1),
            tall,
            preferred_element_type=jnp.float32,
        )
        outer = lax.dot_general(key_low, value_high, tall, preferred_element_type=jnp.float32)
        outer = outer + both[:, LANES:] + both[:, :LANES]
        outer = jnp.where(keep, outer, 0.0)
        packed = outer[:HDIM]
        for head in range(1, GROUP):
            packed = packed + outer[head * HDIM : (head + 1) * HDIM]
        if tile < full:
            out_ref[tile * HDIM : (tile + 1) * HDIM, :] = packed
        else:
            folded = packed[:fold]
            for part in range(1, GROUP):
                folded = folded + pltpu.roll(
                    packed[part * fold : (part + 1) * fold], part * HDIM, 1
                )
            out_ref[tail : tail + fold, :] = folded
        out_ref[tail + fold + tile : tail + fold + tile + 1, :] = jnp.sum(
            keys, axis=0, keepdims=True
        )


def query_kernel(place_ref, *refs):
    hidden, refs = refs[:TEAM], refs[TEAM:]
    second, refs = refs[:PIECES], refs[PIECES:]
    out_ref, weights_ref, hidden_ref, sems, hidden_s = refs
    tokens = hidden_ref.shape[1]
    copies = load_blocks(place_ref, 16, second, 0, weights_ref, sems)
    hidden_copies = load_hidden(hidden, hidden_ref, hidden_s)
    for copy in copies:
        copy.wait()
    for at in range(TEAM):
        hidden_copies[at].wait()
        rows = slice(at * tokens, (at + 1) * tokens)
        queries = jnp.dot(
            hidden_ref[at], weights_ref[...], preferred_element_type=jnp.float32
        )
        out_ref[rows, :] = jnp.maximum(queries, 0.0)


def attend_kernel(slot_ref, live_ref, query_ref, state_ref, out_ref, factor_ref):
    tokens = query_ref.shape[0]
    tiles = query_ref.shape[1] // LANES
    tail = (tiles - 1) * HDIM
    fold = HDIM // GROUP

    @pl.when(pl.program_id(0) == 0)
    def _():
        same_head = block_mask()
        summed = jnp.sum(state_ref[...], axis=0)
        for tile in range(tiles):
            if tile < tiles - 1:
                packed = summed[tile * HDIM : (tile + 1) * HDIM]
            else:
                folded = summed[tail : tail + fold]
                packed = jnp.concatenate(
                    [folded]
                    + [pltpu.roll(folded, LANES - part * HDIM, 1) for part in range(1, GROUP)],
                    axis=0,
                )
            state = jnp.where(same_head, jnp.concatenate([packed] * GROUP, axis=0), 0.0)
            total = summed[tail + fold + tile : tail + fold + tile + 1]
            total = jnp.transpose(jnp.broadcast_to(total, (LANES, LANES)))
            total = jnp.where(same_head, total, 0.0)
            high, low = halves(jnp.concatenate([state, total], axis=1))
            factor_ref[tile, :, : 2 * LANES] = high
            factor_ref[tile, :, 2 * LANES :] = low

    live = live_rows(live_ref[pl.program_id(0)], tokens)
    for tile in range(tiles):
        high, low = halves(query_ref[:, tile * LANES : (tile + 1) * LANES])
        main = jnp.dot(high, factor_ref[tile], preferred_element_type=jnp.float32)
        small = jnp.dot(
            low, factor_ref[tile, :, : 2 * LANES], preferred_element_type=jnp.float32
        )
        total = main[:, 2 * LANES :] + small + main[:, : 2 * LANES]
        result = total[:, :LANES] / (total[:, LANES:] + attn_eps) * live
        if tile < tiles - 1:
            out_ref[0, tile * tokens : (tile + 1) * tokens, :] = result.astype(jnp.bfloat16)
        else:
            quarter = tokens // GROUP
            folded = result[:quarter]
            for part in range(1, GROUP):
                folded = folded + pltpu.roll(
                    result[part * quarter : (part + 1) * quarter], part * HDIM, 1
                )
            out_ref[0, tile * tokens :, :] = folded.astype(jnp.bfloat16)


def assemble_kernel(packed_ref, out_ref):
    tokens = out_ref.shape[0]
    full = (packed_ref.shape[1] - tokens // GROUP) // tokens
    lane = lax.broadcasted_iota(jnp.int32, (tokens, LANES), 1)
    carried = jnp.zeros((tokens, LANES), jnp.float32)
    for rank in range(TEAM):
        shift = rank * HDIM
        for tile in range(full):
            part = packed_ref[rank, tile * tokens : (tile + 1) * tokens, :].astype(jnp.float32)
            part = part if rank == 0 else pltpu.roll(part, shift, 1)
            at = (rank * full + tile) * LANES
            out_ref[:, at : at + LANES] = jnp.where(lane < shift, carried, part).astype(
                jnp.bfloat16
            )
            carried = part
        folded = packed_ref[rank, full * tokens :, :].astype(jnp.float32)
        pieces = []
        for row in range(GROUP):
            turn = (rank - row) % GROUP * HDIM
            pieces.append(folded if turn == 0 else pltpu.roll(folded, turn, 1))
        edge = jnp.concatenate(pieces, axis=0)
        carried = jnp.where(lane < shift, carried, edge)
    at = TEAM * full * LANES
    out_ref[:, at:] = carried.astype(jnp.bfloat16)


def compute_state(place, live, hidden, first):
    tokens, contraction = hidden[0].shape
    wide = (first[0].shape[2] - LANES) // 2
    tiles = wide // LANES + 1
    slots = -(-((tiles - 1) * HDIM + HDIM // GROUP + tiles) // 8) * 8
    return pl.pallas_call(
        state_kernel,
        in_specs=[SMEM, SMEM] + [HBM] * (TEAM + len(first)),
        out_specs=VMEM,
        out_shape=jax.ShapeDtypeStruct((slots, LANES), jnp.float32),
        scratch_shapes=[
            pltpu.VMEM((TEAM * tokens, wide + LANES), jnp.float32),
            pltpu.VMEM((TEAM * tokens, wide), jnp.float32),
            pltpu.VMEM((contraction, 2 * wide + LANES), jnp.bfloat16),
            pltpu.VMEM((TEAM, tokens, contraction), jnp.bfloat16),
            pltpu.SemaphoreType.DMA((16,)),
            pltpu.SemaphoreType.DMA((TEAM,)),
        ],
        compiler_params=PARAMS,
        name="state",
    )(place, live, *hidden, *first)


def compute_queries(place, hidden, second):
    tokens, contraction = hidden[0].shape
    width = second[0].shape[2]
    return pl.pallas_call(
        query_kernel,
        in_specs=[SMEM] + [HBM] * (TEAM + len(second)),
        out_specs=VMEM,
        out_shape=jax.ShapeDtypeStruct((TEAM * tokens, width), jnp.float32),
        scratch_shapes=[
            pltpu.VMEM((contraction, width), jnp.bfloat16),
            pltpu.VMEM((TEAM, tokens, contraction), jnp.bfloat16),
            pltpu.SemaphoreType.DMA((16,)),
            pltpu.SemaphoreType.DMA((TEAM,)),
        ],
        compiler_params=PARAMS,
        cost_estimate=pl.CostEstimate(
            flops=2 * TEAM * tokens * contraction * width,
            bytes_accessed=4 * TEAM * tokens * width + 2 * contraction * (width + TEAM * tokens),
            transcendentals=0,
        ),
        name="queries",
    )(place, *hidden, *second)


def compute_output(slots, live, queries, state):
    tokens, width = queries.shape[0] // TEAM, queries.shape[1]
    packed = (width // LANES - 1) * tokens + tokens // GROUP
    return pl.pallas_call(
        attend_kernel,
        grid_spec=pltpu.PrefetchScalarGridSpec(
            num_scalar_prefetch=2,
            grid=(TEAM,),
            in_specs=[
                pl.BlockSpec((tokens, width), lambda i, slots, live: (i, 0)),
                pl.BlockSpec(state.shape, lambda i, slots, live: (0, 0, 0)),
            ],
            out_specs=pl.BlockSpec((1, packed, LANES), lambda i, slots, live: (slots[i], 0, 0)),
            scratch_shapes=[pltpu.VMEM((width // LANES, LANES, 4 * LANES), jnp.bfloat16)],
        ),
        out_shape=jax.ShapeDtypeStruct((TEAM, packed, LANES), jnp.bfloat16),
        compiler_params=pltpu.CompilerParams(vmem_limit_bytes=58 * 1024 * 1024),
        name="attend",
    )(slots, live, queries, state)


def spread(block, count, axis, groups):
    copies = jnp.broadcast_to(block[None], (count,) + block.shape)
    return lax.all_to_all(copies, axis, 0, 0, axis_index_groups=groups)


def exchange(block, mask, axis, count):
    return lax.ppermute(block, axis, [(i, i ^ mask) for i in range(count)])


def far_stage(held, one, two, count):
    from_one = exchange(held, one, "img", count)
    from_two = exchange(held, two, "img", count)
    opposite = exchange(from_one, two, "img", count)
    return [held, from_one, from_two, opposite]


def body(tokens, norm_gain, caption, null_caption, keep, bucket_rows, w_qkv):
    grid_rows, grid_cols, features_count = tokens.shape[1:]
    token_count = grid_rows * grid_cols
    seq_size = lax.axis_size("seq")
    img_size = lax.axis_size("img")
    side = 4
    teams = seq_size // TEAM
    seq_at = lax.axis_index("seq")
    img_at = lax.axis_index("img")
    rank = seq_at % TEAM
    same_rank = [[TEAM * j + r for j in range(teams)] for r in range(TEAM)]
    team = [[TEAM * j + r for r in range(TEAM)] for j in range(teams)]
    x_groups = [[y * side + x for x in range(side)] for y in range(side)]
    y_groups = [[y * side + x for y in range(side)] for x in range(side)]
    depth = features_count // img_size
    padded = -(-depth // 16) * 16
    columns = w_qkv.shape[1] * seq_size
    inner = columns // 3
    share = inner // TEAM
    main = share // LANES * LANES
    rest = share - main

    gathered = lax.all_gather(w_qkv, "seq", axis=0)
    rows = jnp.transpose(gathered, (1, 0, 2)).reshape(depth, columns)
    rows = jnp.pad(rows, ((0, padded - depth), (0, 0)))

    def pick(part):
        chosen = rows[:, part * inner : part * inner + share]
        for r in range(1, TEAM):
            start = part * inner + r * share
            chosen = jnp.where(rank == r, rows[:, start : start + share], chosen)
        return chosen

    query_cols, key_cols, value_cols = pick(0), pick(1), pick(2)
    first = jnp.concatenate(
        [
            key_cols[:, :main],
            value_cols[:, :main],
            key_cols[:, main:],
            value_cols[:, main:],
            jnp.zeros((padded, LANES - 2 * rest), jnp.bfloat16),
        ],
        axis=1,
    )
    second = jnp.pad(query_cols, ((0, 0), (0, LANES - rest)))
    first, tokens = lax.optimization_barrier((first, tokens))
    first_near = spread(first, side, "img", x_groups)
    y_at, x_at = img_at // side, img_at % side
    place = jnp.concatenate(
        [
            jnp.bitwise_xor(y_at, FAR_MASKS) * side + NEAR_SLOTS,
            NEAR_SLOTS * side + jnp.bitwise_xor(x_at, FAR_MASKS),
        ]
    ).astype(jnp.int32)
    slots = jnp.bitwise_xor(rank, jnp.arange(TEAM, dtype=jnp.int32))
    first_row = (seq_at - rank + slots) * grid_rows
    live = jnp.clip(bucket_rows[0] - first_row, 0, grid_rows) * grid_cols
    second, first_near, place, live, slots = lax.optimization_barrier(
        (second, first_near, place, live, slots)
    )
    second_near = spread(second, side, "img", y_groups)
    first_pieces = far_stage(first_near, side, 3 * side, img_size)
    second_pieces = far_stage(second_near, 1, 3, img_size)
    features = jnp.transpose(tokens[0], (0, 2, 1)).astype(jnp.float32)
    mean_square = jnp.mean(features * features, axis=1, keepdims=True)
    condition = jnp.where(keep[0] > 0, caption[0], null_caption).astype(jnp.float32)
    hidden = (
        features * lax.rsqrt(mean_square + norm_eps) * norm_gain.astype(jnp.float32)[None, :, None]
        + condition[None, :, None]
    ).astype(jnp.bfloat16)
    hidden = hidden.reshape(grid_rows, img_size, depth, grid_cols)
    hidden = jnp.pad(hidden, ((0, 0), (0, 0), (0, padded - depth), (0, 0)))
    hidden = hidden.reshape(grid_rows, img_size * padded, grid_cols)
    mine = jnp.transpose(hidden, (0, 2, 1)).reshape(token_count, img_size * padded)
    beside = exchange(mine, 2, "seq", seq_size)
    late, _ = lax.optimization_barrier((beside, first_pieces[1:3]))
    across = exchange(late, 1, "seq", seq_size)
    hidden = (mine, exchange(mine, 1, "seq", seq_size), beside, across)

    part = compute_state(place, live, hidden, first_pieces)
    state = spread(part, teams, "seq", same_rank)
    queries = compute_queries(place, hidden, second_pieces)

    result = compute_output(slots, live, queries, state)
    result = lax.all_to_all(result, "seq", 0, 0, axis_index_groups=team)
    result = pl.pallas_call(
        assemble_kernel,
        in_specs=[VMEM],
        out_specs=VMEM,
        out_shape=jax.ShapeDtypeStruct((token_count, inner), jnp.bfloat16),
        compiler_params=pltpu.CompilerParams(vmem_limit_bytes=16 * 1024 * 1024),
        name="assemble",
    )(result)
    return result.reshape(1, grid_rows, grid_cols, inner)


def solution(mesh):
    in_specs = (
        P("img", "seq", None, None),
        P(),
        P("img", None),
        P(),
        P("img"),
        P("img"),
        P("img", "seq"),
    )
    out_specs = P("img", "seq", None, None)

    return jax.shard_map(
        body, mesh=mesh, in_specs=in_specs, out_specs=out_specs, check_vma=False
    )
```

```python
import functools

import jax
import jax.numpy as jnp
import numpy as np
from jax import lax
from jax.experimental import pallas as pl
from jax.experimental.pallas import tpu as pltpu
from jax.sharding import PartitionSpec as P


HDIM = 32
LANES = 128
GROUP = LANES // HDIM
TEAM = 4

norm_eps = 1e-06
attn_eps = 1e-06

VMEM = pl.BlockSpec(memory_space=pltpu.VMEM)
SMEM = pl.BlockSpec(memory_space=pltpu.SMEM)
HBM = pl.BlockSpec(memory_space=pl.ANY)
PARAMS = pltpu.CompilerParams(vmem_limit_bytes=32 * 1024 * 1024)

FAR_MASKS = np.array([0] * 4 + [1] * 4 + [3] * 4 + [2] * 4)
NEAR_SLOTS = np.array([0, 1, 2, 3] * 4)
PIECES = 4


def block_mask():
    row = lax.broadcasted_iota(jnp.int32, (LANES, LANES), 0) // HDIM
    col = lax.broadcasted_iota(jnp.int32, (LANES, LANES), 1) // HDIM
    return row == col


def live_rows(limit, tokens):
    token = lax.broadcasted_iota(jnp.int32, (tokens, LANES), 0)
    return (token < limit).astype(jnp.float32)


def halves(value):
    high = value.astype(jnp.bfloat16)
    return high, (value - high.astype(jnp.float32)).astype(jnp.bfloat16)


def load_blocks(place_ref, base, pieces, start, into_ref, sems):
    depth, width = pieces[0].shape[1], into_ref.shape[1]
    copies = []
    for piece in pieces:
        for at in range(piece.shape[0]):
            count = len(copies)
            row = pl.multiple_of(place_ref[base + count] * depth, 16)
            copies.append(
                pltpu.make_async_copy(
                    piece.at[at, :, pl.ds(start, width)],
                    into_ref.at[pl.ds(row, depth), :],
                    sems.at[count],
                )
            )
    for copy in copies:
        copy.start()
    return copies


def load_hidden(hidden, into_ref, sems):
    copies = [
        pltpu.make_async_copy(ref, into_ref.at[at], sems.at[at])
        for at, ref in enumerate(hidden)
    ]
    for copy in copies:
        copy.start()
    return copies


def layout_kernel(plan, rank_ref, gathered_ref, first_ref, second_ref):
    depth = gathered_ref.shape[1]
    rows = first_ref.shape[1]
    lane = lax.broadcasted_iota(jnp.int32, (depth, LANES), 1)
    for rank, tiles in enumerate(plan):

        @pl.when(rank_ref[0] == rank)
        def _(tiles=tiles):
            for out_ref, at, pieces in (
                (first_ref if which == 0 else second_ref, tile, parts)
                for which, tile, parts in tiles
            ):
                value = jnp.zeros((depth, LANES), jnp.float32)
                for shard, source, target, size in pieces:
                    part = gathered_ref[shard].astype(jnp.float32)
                    part = jnp.concatenate(
                        [part, jnp.zeros((depth, LANES - part.shape[1]), jnp.float32)], axis=1
                    )
                    turn = (target - source) % LANES
                    part = part if turn == 0 else pltpu.roll(part, turn, 1)
                    inside = jnp.logical_and(lane >= target, lane < target + size)
                    value = jnp.where(inside, part, value)
                value = jnp.concatenate(
                    [value, jnp.zeros((rows - depth, LANES), jnp.float32)], axis=0
                ).astype(jnp.bfloat16)
                for copy in range(out_ref.shape[0]):
                    out_ref[copy, :, at * LANES : (at + 1) * LANES] = value


def layout_plan(shard, inner, share, main):
    plan = []
    for rank in range(TEAM):
        query, key, value = (part * inner + rank * share for part in range(3))
        rest = share - main
        spans = [
            (0, 0, key, main),
            (0, main, value, main),
            (0, 2 * main, key + main, rest),
            (0, 2 * main + rest, value + main, rest),
            (1, 0, query, share),
        ]
        tiles = {}
        for which, target, source, size in spans:
            while size:
                step = min(size, LANES - target % LANES, shard - source % shard)
                tiles.setdefault((which, target // LANES), []).append(
                    (source // shard, source % shard, target % LANES, step)
                )
                target, source, size = target + step, source + step, size - step
        plan.append([(which, tile, parts) for (which, tile), parts in sorted(tiles.items())])
    return plan


def state_kernel(place_ref, live_ref, *refs):
    hidden, first, refs = refs[:TEAM], refs[TEAM : TEAM + PIECES], refs[TEAM + PIECES :]
    out_ref, keys_ref, values_ref, weights_ref, hidden_ref, sems, hidden_s = refs
    tokens = hidden_ref.shape[1]
    full = values_ref.shape[1] // LANES
    copies = load_blocks(place_ref, 0, first, 0, weights_ref, sems)
    hidden_copies = load_hidden(hidden, hidden_ref, hidden_s)
    for copy in copies:
        copy.wait()
    wide = full * LANES
    for at in range(TEAM):
        hidden_copies[at].wait()
        rows = slice(at * tokens, (at + 1) * tokens)
        block = hidden_ref[at]
        live = live_rows(live_ref[at], tokens)
        keys = jnp.dot(block, weights_ref[:, :wide], preferred_element_type=jnp.float32)
        for tile in range(full):
            lanes = slice(tile * LANES, (tile + 1) * LANES)
            keys_ref[rows, lanes] = jnp.maximum(keys[:, lanes], 0.0) * live
        values_ref[rows, :] = jnp.dot(
            block, weights_ref[:, wide : 2 * wide], preferred_element_type=jnp.float32
        )
        keys_ref[rows, wide:] = jnp.dot(
            block, weights_ref[:, 2 * wide :], preferred_element_type=jnp.float32
        )
    same_head = block_mask()
    column = lax.broadcasted_iota(jnp.int32, (LANES, LANES), 1)
    tiles = full + 1
    tail = full * HDIM
    fold = HDIM // GROUP
    lines = [None] * tiles
    totals = [None] * tiles
    for tile in range(tiles):
        keys = keys_ref[:, tile * LANES : (tile + 1) * LANES]
        if tile < full:
            values = values_ref[:, tile * LANES : (tile + 1) * LANES]
            keep = same_head
        else:
            values = pltpu.roll(keys, LANES - HDIM, 1)
            live = jnp.concatenate(
                [live_rows(live_ref[at], tokens) for at in range(TEAM)], axis=0
            )
            keys = jnp.maximum(keys, 0.0) * live
            keep = jnp.logical_and(same_head, column < HDIM)
        key_high, key_low = halves(keys)
        value_high, value_low = halves(values)
        tall = (((0,), (0,)), ((), ()))
        both = lax.dot_general(
            key_high,
            jnp.concatenate([value_high, value_low], axis=1),
            tall,
            preferred_element_type=jnp.float32,
        )
        outer = lax.dot_general(key_low, value_high, tall, preferred_element_type=jnp.float32)
        outer = outer + both[:, LANES:] + both[:, :LANES]
        outer = jnp.where(keep, outer, 0.0)
        packed = outer[:HDIM]
        for head in range(1, GROUP):
            packed = packed + outer[head * HDIM : (head + 1) * HDIM]
        if tile == full:
            folded = packed[:fold]
            for part in range(1, GROUP):
                folded = folded + pltpu.roll(
                    packed[part * fold : (part + 1) * fold], part * HDIM, 1
                )
            packed = folded
        lines[tile] = packed
        totals[tile] = jnp.sum(keys, axis=0, keepdims=True)
    used = tail + fold + tiles
    spare = jnp.zeros((out_ref.shape[1] - used, LANES), jnp.float32)
    block = jnp.concatenate(lines + totals + [spare], axis=0)
    for copy in range(out_ref.shape[0]):
        out_ref[copy] = block


def query_kernel(place_ref, *refs):
    hidden, refs = refs[:TEAM], refs[TEAM:]
    second, refs = refs[:PIECES], refs[PIECES:]
    out_ref, weights_ref, hidden_ref, sems, hidden_s = refs
    tokens = hidden_ref.shape[1]
    copies = load_blocks(place_ref, 16, second, 0, weights_ref, sems)
    hidden_copies = load_hidden(hidden, hidden_ref, hidden_s)
    for copy in copies:
        copy.wait()
    for at in range(TEAM):
        hidden_copies[at].wait()
        rows = slice(at * tokens, (at + 1) * tokens)
        queries = jnp.dot(
            hidden_ref[at], weights_ref[...], preferred_element_type=jnp.float32
        )
        out_ref[rows, :] = jnp.maximum(queries, 0.0)


def attend_kernel(slot_ref, live_ref, query_ref, state_ref, out_ref, factor_ref):
    tokens = query_ref.shape[0]
    tiles = query_ref.shape[1] // LANES
    tail = (tiles - 1) * HDIM
    fold = HDIM // GROUP

    @pl.when(pl.program_id(0) == 0)
    def _():
        same_head = block_mask()
        summed = jnp.sum(state_ref[...], axis=0)
        for tile in range(tiles):
            if tile < tiles - 1:
                packed = summed[tile * HDIM : (tile + 1) * HDIM]
            else:
                folded = summed[tail : tail + fold]
                packed = jnp.concatenate(
                    [folded]
                    + [pltpu.roll(folded, LANES - part * HDIM, 1) for part in range(1, GROUP)],
                    axis=0,
                )
            state = jnp.where(same_head, jnp.concatenate([packed] * GROUP, axis=0), 0.0)
            total = summed[tail + fold + tile : tail + fold + tile + 1]
            total = jnp.transpose(jnp.broadcast_to(total, (LANES, LANES)))
            total = jnp.where(same_head, total, 0.0)
            high, low = halves(jnp.concatenate([state, total], axis=1))
            factor_ref[tile, :, : 2 * LANES] = high
            factor_ref[tile, :, 2 * LANES :] = low

    live = live_rows(live_ref[pl.program_id(0)], tokens)
    for tile in range(tiles):
        high, low = halves(query_ref[:, tile * LANES : (tile + 1) * LANES])
        main = jnp.dot(high, factor_ref[tile], preferred_element_type=jnp.float32)
        small = jnp.dot(
            low, factor_ref[tile, :, : 2 * LANES], preferred_element_type=jnp.float32
        )
        total = main[:, 2 * LANES :] + small + main[:, : 2 * LANES]
        result = total[:, :LANES] / (total[:, LANES:] + attn_eps) * live
        if tile < tiles - 1:
            out_ref[0, tile * tokens : (tile + 1) * tokens, :] = result.astype(jnp.bfloat16)
        else:
            quarter = tokens // GROUP
            folded = result[:quarter]
            for part in range(1, GROUP):
                folded = folded + pltpu.roll(
                    result[part * quarter : (part + 1) * quarter], part * HDIM, 1
                )
            out_ref[0, tile * tokens :, :] = folded.astype(jnp.bfloat16)


def assemble_kernel(packed_ref, out_ref):
    tokens = out_ref.shape[0]
    full = (packed_ref.shape[1] - tokens // GROUP) // tokens
    lane = lax.broadcasted_iota(jnp.int32, (tokens, LANES), 1)
    carried = jnp.zeros((tokens, LANES), jnp.float32)
    for rank in range(TEAM):
        shift = rank * HDIM
        for tile in range(full):
            part = packed_ref[rank, tile * tokens : (tile + 1) * tokens, :].astype(jnp.float32)
            part = part if rank == 0 else pltpu.roll(part, shift, 1)
            at = (rank * full + tile) * LANES
            out_ref[:, at : at + LANES] = jnp.where(lane < shift, carried, part).astype(
                jnp.bfloat16
            )
            carried = part
        folded = packed_ref[rank, full * tokens :, :].astype(jnp.float32)
        pieces = []
        for row in range(GROUP):
            turn = (rank - row) % GROUP * HDIM
            pieces.append(folded if turn == 0 else pltpu.roll(folded, turn, 1))
        edge = jnp.concatenate(pieces, axis=0)
        carried = jnp.where(lane < shift, carried, edge)
    at = TEAM * full * LANES
    out_ref[:, at:] = carried.astype(jnp.bfloat16)


def compute_state(place, live, hidden, first, copies):
    tokens, contraction = hidden[0].shape
    wide = (first[0].shape[2] - LANES) // 2
    tiles = wide // LANES + 1
    slots = -(-((tiles - 1) * HDIM + HDIM // GROUP + tiles) // 8) * 8
    return pl.pallas_call(
        state_kernel,
        in_specs=[SMEM, SMEM] + [HBM] * (TEAM + len(first)),
        out_specs=VMEM,
        out_shape=jax.ShapeDtypeStruct((copies, slots, LANES), jnp.float32),
        scratch_shapes=[
            pltpu.VMEM((TEAM * tokens, wide + LANES), jnp.float32),
            pltpu.VMEM((TEAM * tokens, wide), jnp.float32),
            pltpu.VMEM((contraction, 2 * wide + LANES), jnp.bfloat16),
            pltpu.VMEM((TEAM, tokens, contraction), jnp.bfloat16),
            pltpu.SemaphoreType.DMA((16,)),
            pltpu.SemaphoreType.DMA((TEAM,)),
        ],
        compiler_params=PARAMS,
        name="state",
    )(place, live, *hidden, *first)


def compute_queries(place, hidden, second):
    tokens, contraction = hidden[0].shape
    width = second[0].shape[2]
    return pl.pallas_call(
        query_kernel,
        in_specs=[SMEM] + [HBM] * (TEAM + len(second)),
        out_specs=VMEM,
        out_shape=jax.ShapeDtypeStruct((TEAM * tokens, width), jnp.float32),
        scratch_shapes=[
            pltpu.VMEM((contraction, width), jnp.bfloat16),
            pltpu.VMEM((TEAM, tokens, contraction), jnp.bfloat16),
            pltpu.SemaphoreType.DMA((16,)),
            pltpu.SemaphoreType.DMA((TEAM,)),
        ],
        compiler_params=PARAMS,
        cost_estimate=pl.CostEstimate(
            flops=2 * TEAM * tokens * contraction * width,
            bytes_accessed=4 * TEAM * tokens * width + 2 * contraction * (width + TEAM * tokens),
            transcendentals=0,
        ),
        name="queries",
    )(place, *hidden, *second)


def compute_output(slots, live, queries, state):
    tokens, width = queries.shape[0] // TEAM, queries.shape[1]
    packed = (width // LANES - 1) * tokens + tokens // GROUP
    return pl.pallas_call(
        attend_kernel,
        grid_spec=pltpu.PrefetchScalarGridSpec(
            num_scalar_prefetch=2,
            grid=(TEAM,),
            in_specs=[
                pl.BlockSpec((tokens, width), lambda i, slots, live: (i, 0)),
                pl.BlockSpec(state.shape, lambda i, slots, live: (0, 0, 0)),
            ],
            out_specs=pl.BlockSpec((1, packed, LANES), lambda i, slots, live: (slots[i], 0, 0)),
            scratch_shapes=[pltpu.VMEM((width // LANES, LANES, 4 * LANES), jnp.bfloat16)],
        ),
        out_shape=jax.ShapeDtypeStruct((TEAM, packed, LANES), jnp.bfloat16),
        compiler_params=pltpu.CompilerParams(vmem_limit_bytes=58 * 1024 * 1024),
        name="attend",
    )(slots, live, queries, state)


def exchange(block, mask, axis, count):
    return lax.ppermute(block, axis, [(i, i ^ mask) for i in range(count)])


def far_stage(held, one, two, count):
    from_one = exchange(held, one, "img", count)
    from_two = exchange(held, two, "img", count)
    opposite = exchange(from_one, two, "img", count)
    return [held, from_one, from_two, opposite]


def body(tokens, norm_gain, caption, null_caption, keep, bucket_rows, w_qkv):
    grid_rows, grid_cols, features_count = tokens.shape[1:]
    token_count = grid_rows * grid_cols
    seq_size = lax.axis_size("seq")
    img_size = lax.axis_size("img")
    side = 4
    teams = seq_size // TEAM
    seq_at = lax.axis_index("seq")
    img_at = lax.axis_index("img")
    rank = seq_at % TEAM
    same_rank = [[TEAM * j + r for j in range(teams)] for r in range(TEAM)]
    team = [[TEAM * j + r for r in range(TEAM)] for j in range(teams)]
    x_groups = [[y * side + x for x in range(side)] for y in range(side)]
    y_groups = [[y * side + x for y in range(side)] for x in range(side)]
    depth = features_count // img_size
    padded = -(-depth // 16) * 16
    columns = w_qkv.shape[1] * seq_size
    inner = columns // 3
    share = inner // TEAM
    main = share // LANES * LANES

    gathered = lax.all_gather(w_qkv, "seq", axis=0)
    wide = 2 * main + LANES
    first, second = pl.pallas_call(
        functools.partial(layout_kernel, layout_plan(w_qkv.shape[1], inner, share, main)),
        in_specs=[SMEM, VMEM],
        out_specs=[VMEM, VMEM],
        out_shape=[
            jax.ShapeDtypeStruct((side, padded, wide), jnp.bfloat16),
            jax.ShapeDtypeStruct((side, padded, main + LANES), jnp.bfloat16),
        ],
        compiler_params=pltpu.CompilerParams(vmem_limit_bytes=16 * 1024 * 1024),
        name="layout",
    )(rank.reshape(1).astype(jnp.int32), gathered)
    first, tokens = lax.optimization_barrier((first, tokens))
    first_near = lax.all_to_all(first, "img", 0, 0, axis_index_groups=x_groups)
    y_at, x_at = img_at // side, img_at % side
    place = jnp.concatenate(
        [
            jnp.bitwise_xor(y_at, FAR_MASKS) * side + NEAR_SLOTS,
            NEAR_SLOTS * side + jnp.bitwise_xor(x_at, FAR_MASKS),
        ]
    ).astype(jnp.int32)
    slots = jnp.bitwise_xor(rank, jnp.arange(TEAM, dtype=jnp.int32))
    first_row = (seq_at - rank + slots) * grid_rows
    live = jnp.clip(bucket_rows[0] - first_row, 0, grid_rows) * grid_cols
    second, first_near, place, live, slots = lax.optimization_barrier(
        (second, first_near, place, live, slots)
    )
    second_near = lax.all_to_all(second, "img", 0, 0, axis_index_groups=y_groups)
    first_pieces = far_stage(first_near, side, 3 * side, img_size)
    second_pieces = far_stage(second_near, 1, 3, img_size)
    features = jnp.transpose(tokens[0], (0, 2, 1)).astype(jnp.float32)
    mean_square = jnp.mean(features * features, axis=1, keepdims=True)
    condition = jnp.where(keep[0] > 0, caption[0], null_caption).astype(jnp.float32)
    hidden = (
        features * lax.rsqrt(mean_square + norm_eps) * norm_gain.astype(jnp.float32)[None, :, None]
        + condition[None, :, None]
    ).astype(jnp.bfloat16)
    hidden = hidden.reshape(grid_rows, img_size, depth, grid_cols)
    hidden = jnp.pad(hidden, ((0, 0), (0, 0), (0, padded - depth), (0, 0)))
    hidden = hidden.reshape(grid_rows, img_size * padded, grid_cols)
    mine = jnp.transpose(hidden, (0, 2, 1)).reshape(token_count, img_size * padded)
    beside = exchange(mine, 2, "seq", seq_size)
    late, _ = lax.optimization_barrier((beside, first_pieces[1:3]))
    across = exchange(late, 1, "seq", seq_size)
    hidden = (mine, exchange(mine, 1, "seq", seq_size), beside, across)

    part = compute_state(place, live, hidden, first_pieces, teams)
    state = lax.all_to_all(part, "seq", 0, 0, axis_index_groups=same_rank)
    queries = compute_queries(place, hidden, second_pieces)

    result = compute_output(slots, live, queries, state)
    result = lax.all_to_all(result, "seq", 0, 0, axis_index_groups=team)
    result = pl.pallas_call(
        assemble_kernel,
        in_specs=[VMEM],
        out_specs=VMEM,
        out_shape=jax.ShapeDtypeStruct((token_count, inner), jnp.bfloat16),
        compiler_params=pltpu.CompilerParams(vmem_limit_bytes=16 * 1024 * 1024),
        name="assemble",
    )(result)
    return result.reshape(1, grid_rows, grid_cols, inner)


def solution(mesh):
    in_specs = (
        P("img", "seq", None, None),
        P(),
        P("img", None),
        P(),
        P("img"),
        P("img"),
        P("img", "seq"),
    )
    out_specs = P("img", "seq", None, None)

    return jax.shard_map(body, mesh=mesh, in_specs=in_specs, out_specs=out_specs, check_vma=False)
```

```python
import functools

import jax
import jax.numpy as jnp
import numpy as np
from jax import lax
from jax.experimental import pallas as pl
from jax.experimental.pallas import tpu as pltpu
from jax.sharding import PartitionSpec as P


HDIM = 32
LANES = 128
GROUP = LANES // HDIM
TEAM = 4

norm_eps = 1e-06
attn_eps = 1e-06

VMEM = pl.BlockSpec(memory_space=pltpu.VMEM)
SMEM = pl.BlockSpec(memory_space=pltpu.SMEM)
HBM = pl.BlockSpec(memory_space=pl.ANY)
PARAMS = pltpu.CompilerParams(vmem_limit_bytes=32 * 1024 * 1024)

FAR_MASKS = np.array([0] * 4 + [1] * 4 + [3] * 4 + [2] * 4)
NEAR_SLOTS = np.array([0, 1, 2, 3] * 4)
PIECES = 4


def block_mask():
    row = lax.broadcasted_iota(jnp.int32, (LANES, LANES), 0) // HDIM
    col = lax.broadcasted_iota(jnp.int32, (LANES, LANES), 1) // HDIM
    return row == col


def live_rows(limit, tokens):
    token = lax.broadcasted_iota(jnp.int32, (tokens, LANES), 0)
    return (token < limit).astype(jnp.float32)


def halves(value):
    high = value.astype(jnp.bfloat16)
    return high, (value - high.astype(jnp.float32)).astype(jnp.bfloat16)


def load_blocks(place_ref, base, pieces, start, into_ref, sems):
    depth, width = pieces[0].shape[1], into_ref.shape[1]
    copies = []
    for piece in pieces:
        for at in range(piece.shape[0]):
            count = len(copies)
            row = pl.multiple_of(place_ref[base + count] * depth, 16)
            copies.append(
                pltpu.make_async_copy(
                    piece.at[at, :, pl.ds(start, width)],
                    into_ref.at[pl.ds(row, depth), :],
                    sems.at[count],
                )
            )
    for copy in copies:
        copy.start()
    return copies


def load_hidden(hidden, into_ref, sems):
    copies = [
        pltpu.make_async_copy(ref, into_ref.at[at], sems.at[at])
        for at, ref in enumerate(hidden)
    ]
    for copy in copies:
        copy.start()
    return copies


def layout_kernel(plan, rank_ref, gathered_ref, first_ref, second_ref):
    depth = gathered_ref.shape[1]
    rows = first_ref.shape[1]
    lane = lax.broadcasted_iota(jnp.int32, (depth, LANES), 1)
    for rank, tiles in enumerate(plan):

        @pl.when(rank_ref[0] == rank)
        def _(tiles=tiles):
            for out_ref, at, pieces in (
                (first_ref if which == 0 else second_ref, tile, parts)
                for which, tile, parts in tiles
            ):
                value = jnp.zeros((depth, LANES), jnp.float32)
                for shard, source, target, size in pieces:
                    part = gathered_ref[shard].astype(jnp.float32)
                    part = jnp.concatenate(
                        [part, jnp.zeros((depth, LANES - part.shape[1]), jnp.float32)], axis=1
                    )
                    turn = (target - source) % LANES
                    part = part if turn == 0 else pltpu.roll(part, turn, 1)
                    inside = jnp.logical_and(lane >= target, lane < target + size)
                    value = jnp.where(inside, part, value)
                value = jnp.concatenate(
                    [value, jnp.zeros((rows - depth, LANES), jnp.float32)], axis=0
                ).astype(jnp.bfloat16)
                for copy in range(out_ref.shape[0]):
                    out_ref[copy, :, at * LANES : (at + 1) * LANES] = value


def layout_plan(shard, inner, share, main):
    plan = []
    for rank in range(TEAM):
        query, key, value = (part * inner + rank * share for part in range(3))
        rest = share - main
        spans = [
            (0, 0, key, main),
            (0, main, value, main),
            (0, 2 * main, key + main, rest),
            (0, 2 * main + rest, value + main, rest),
            (1, 0, query, share),
        ]
        tiles = {}
        for which, target, source, size in spans:
            while size:
                step = min(size, LANES - target % LANES, shard - source % shard)
                tiles.setdefault((which, target // LANES), []).append(
                    (source // shard, source % shard, target % LANES, step)
                )
                target, source, size = target + step, source + step, size - step
        plan.append([(which, tile, parts) for (which, tile), parts in sorted(tiles.items())])
    return plan


def state_kernel(place_ref, live_ref, *refs):
    hidden, first, refs = refs[:TEAM], refs[TEAM : TEAM + PIECES], refs[TEAM + PIECES :]
    out_ref, keys_ref, values_ref, weights_ref, hidden_ref, sems, hidden_s = refs
    tokens = hidden_ref.shape[1]
    full = values_ref.shape[1] // LANES
    copies = load_blocks(place_ref, 0, first, 0, weights_ref, sems)
    hidden_copies = load_hidden(hidden, hidden_ref, hidden_s)
    for copy in copies:
        copy.wait()
    wide = full * LANES
    for at in range(TEAM):
        hidden_copies[at].wait()
        rows = slice(at * tokens, (at + 1) * tokens)
        block = hidden_ref[at]
        live = live_rows(live_ref[at], tokens)
        keys = jnp.dot(block, weights_ref[:, :wide], preferred_element_type=jnp.float32)
        for tile in range(full):
            lanes = slice(tile * LANES, (tile + 1) * LANES)
            keys_ref[rows, lanes] = jnp.maximum(keys[:, lanes], 0.0) * live
        values_ref[rows, :] = jnp.dot(
            block, weights_ref[:, wide : 2 * wide], preferred_element_type=jnp.float32
        )
        keys_ref[rows, wide:] = jnp.dot(
            block, weights_ref[:, 2 * wide :], preferred_element_type=jnp.float32
        )
    same_head = block_mask()
    column = lax.broadcasted_iota(jnp.int32, (LANES, LANES), 1)
    tiles = full + 1
    tail = full * HDIM
    fold = HDIM // GROUP
    lines = [None] * tiles
    totals = [None] * tiles
    for tile in range(tiles):
        keys = keys_ref[:, tile * LANES : (tile + 1) * LANES]
        if tile < full:
            values = values_ref[:, tile * LANES : (tile + 1) * LANES]
            keep = same_head
        else:
            values = pltpu.roll(keys, LANES - HDIM, 1)
            live = jnp.concatenate(
                [live_rows(live_ref[at], tokens) for at in range(TEAM)], axis=0
            )
            keys = jnp.maximum(keys, 0.0) * live
            keep = jnp.logical_and(same_head, column < HDIM)
        key_high, key_low = halves(keys)
        value_high, value_low = halves(values)
        tall = (((0,), (0,)), ((), ()))
        both = lax.dot_general(
            key_high,
            jnp.concatenate([value_high, value_low], axis=1),
            tall,
            preferred_element_type=jnp.float32,
        )
        outer = lax.dot_general(key_low, value_high, tall, preferred_element_type=jnp.float32)
        outer = outer + both[:, LANES:] + both[:, :LANES]
        outer = jnp.where(keep, outer, 0.0)
        packed = outer[:HDIM]
        for head in range(1, GROUP):
            packed = packed + outer[head * HDIM : (head + 1) * HDIM]
        if tile == full:
            folded = packed[:fold]
            for part in range(1, GROUP):
                folded = folded + pltpu.roll(
                    packed[part * fold : (part + 1) * fold], part * HDIM, 1
                )
            packed = folded
        lines[tile] = packed
        totals[tile] = jnp.sum(keys, axis=0, keepdims=True)
    used = tail + fold + tiles
    spare = jnp.zeros((out_ref.shape[1] - used, LANES), jnp.float32)
    block = jnp.concatenate(lines + totals + [spare], axis=0)
    for copy in range(out_ref.shape[0]):
        out_ref[copy] = block


def query_kernel(place_ref, *refs):
    hidden, refs = refs[:TEAM], refs[TEAM:]
    second, refs = refs[:PIECES], refs[PIECES:]
    out_ref, weights_ref, hidden_ref, sems, hidden_s = refs
    tokens = hidden_ref.shape[1]
    copies = load_blocks(place_ref, 16, second, 0, weights_ref, sems)
    hidden_copies = load_hidden(hidden, hidden_ref, hidden_s)
    for copy in copies:
        copy.wait()
    for at in range(TEAM):
        hidden_copies[at].wait()
        rows = slice(at * tokens, (at + 1) * tokens)
        queries = jnp.dot(
            hidden_ref[at], weights_ref[...], preferred_element_type=jnp.float32
        )
        out_ref[rows, :] = jnp.maximum(queries, 0.0)


def attend_kernel(slot_ref, live_ref, query_ref, state_ref, out_ref, factor_ref):
    tokens = query_ref.shape[0]
    tiles = query_ref.shape[1] // LANES
    tail = (tiles - 1) * HDIM
    fold = HDIM // GROUP

    @pl.when(pl.program_id(0) == 0)
    def _():
        same_head = block_mask()
        summed = jnp.sum(state_ref[...], axis=0)
        for tile in range(tiles):
            if tile < tiles - 1:
                packed = summed[tile * HDIM : (tile + 1) * HDIM]
            else:
                folded = summed[tail : tail + fold]
                packed = jnp.concatenate(
                    [folded]
                    + [pltpu.roll(folded, LANES - part * HDIM, 1) for part in range(1, GROUP)],
                    axis=0,
                )
            state = jnp.where(same_head, jnp.concatenate([packed] * GROUP, axis=0), 0.0)
            total = summed[tail + fold + tile : tail + fold + tile + 1]
            total = jnp.transpose(jnp.broadcast_to(total, (LANES, LANES)))
            total = jnp.where(same_head, total, 0.0)
            high, low = halves(jnp.concatenate([state, total], axis=1))
            factor_ref[tile, :, : 2 * LANES] = high
            factor_ref[tile, :, 2 * LANES :] = low

    live = live_rows(live_ref[pl.program_id(0)], tokens)
    for tile in range(tiles):
        high, low = halves(query_ref[:, tile * LANES : (tile + 1) * LANES])
        main = jnp.dot(high, factor_ref[tile], preferred_element_type=jnp.float32)
        small = jnp.dot(
            low, factor_ref[tile, :, : 2 * LANES], preferred_element_type=jnp.float32
        )
        total = main[:, 2 * LANES :] + small + main[:, : 2 * LANES]
        result = total[:, :LANES] / (total[:, LANES:] + attn_eps) * live
        if tile < tiles - 1:
            out_ref[0, tile * tokens : (tile + 1) * tokens, :] = result.astype(jnp.bfloat16)
        else:
            quarter = tokens // GROUP
            folded = result[:quarter]
            for part in range(1, GROUP):
                folded = folded + pltpu.roll(
                    result[part * quarter : (part + 1) * quarter], part * HDIM, 1
                )
            out_ref[0, tile * tokens :, :] = folded.astype(jnp.bfloat16)


def assemble_kernel(packed_ref, out_ref):
    tokens = out_ref.shape[0]
    full = (packed_ref.shape[1] - tokens // GROUP) // tokens
    lane = lax.broadcasted_iota(jnp.int32, (tokens, LANES), 1)
    carried = jnp.zeros((tokens, LANES), jnp.float32)
    for rank in range(TEAM):
        shift = rank * HDIM
        for tile in range(full):
            part = packed_ref[rank, tile * tokens : (tile + 1) * tokens, :].astype(jnp.float32)
            part = part if rank == 0 else pltpu.roll(part, shift, 1)
            at = (rank * full + tile) * LANES
            out_ref[:, at : at + LANES] = jnp.where(lane < shift, carried, part).astype(
                jnp.bfloat16
            )
            carried = part
        folded = packed_ref[rank, full * tokens :, :].astype(jnp.float32)
        pieces = []
        for row in range(GROUP):
            turn = (rank - row) % GROUP * HDIM
            pieces.append(folded if turn == 0 else pltpu.roll(folded, turn, 1))
        edge = jnp.concatenate(pieces, axis=0)
        carried = jnp.where(lane < shift, carried, edge)
    at = TEAM * full * LANES
    out_ref[:, at:] = carried.astype(jnp.bfloat16)


def compute_state(place, live, hidden, first, copies):
    tokens, contraction = hidden[0].shape
    wide = (first[0].shape[2] - LANES) // 2
    tiles = wide // LANES + 1
    slots = -(-((tiles - 1) * HDIM + HDIM // GROUP + tiles) // 8) * 8
    return pl.pallas_call(
        state_kernel,
        in_specs=[SMEM, SMEM] + [HBM] * (TEAM + len(first)),
        out_specs=VMEM,
        out_shape=jax.ShapeDtypeStruct((copies, slots, LANES), jnp.float32),
        scratch_shapes=[
            pltpu.VMEM((TEAM * tokens, wide + LANES), jnp.float32),
            pltpu.VMEM((TEAM * tokens, wide), jnp.float32),
            pltpu.VMEM((contraction, 2 * wide + LANES), jnp.bfloat16),
            pltpu.VMEM((TEAM, tokens, contraction), jnp.bfloat16),
            pltpu.SemaphoreType.DMA((16,)),
            pltpu.SemaphoreType.DMA((TEAM,)),
        ],
        compiler_params=PARAMS,
        name="state",
    )(place, live, *hidden, *first)


def compute_queries(place, hidden, second):
    tokens, contraction = hidden[0].shape
    width = second[0].shape[2]
    return pl.pallas_call(
        query_kernel,
        in_specs=[SMEM] + [HBM] * (TEAM + len(second)),
        out_specs=VMEM,
        out_shape=jax.ShapeDtypeStruct((TEAM * tokens, width), jnp.float32),
        scratch_shapes=[
            pltpu.VMEM((contraction, width), jnp.bfloat16),
            pltpu.VMEM((TEAM, tokens, contraction), jnp.bfloat16),
            pltpu.SemaphoreType.DMA((16,)),
            pltpu.SemaphoreType.DMA((TEAM,)),
        ],
        compiler_params=PARAMS,
        cost_estimate=pl.CostEstimate(
            flops=2 * TEAM * tokens * contraction * width,
            bytes_accessed=4 * TEAM * tokens * width + 2 * contraction * (width + TEAM * tokens),
            transcendentals=0,
        ),
        name="queries",
    )(place, *hidden, *second)


def compute_output(slots, live, queries, state):
    tokens, width = queries.shape[0] // TEAM, queries.shape[1]
    packed = (width // LANES - 1) * tokens + tokens // GROUP
    return pl.pallas_call(
        attend_kernel,
        grid_spec=pltpu.PrefetchScalarGridSpec(
            num_scalar_prefetch=2,
            grid=(TEAM,),
            in_specs=[
                pl.BlockSpec((tokens, width), lambda i, slots, live: (i, 0)),
                pl.BlockSpec(state.shape, lambda i, slots, live: (0, 0, 0)),
            ],
            out_specs=pl.BlockSpec((1, packed, LANES), lambda i, slots, live: (slots[i], 0, 0)),
            scratch_shapes=[pltpu.VMEM((width // LANES, LANES, 4 * LANES), jnp.bfloat16)],
        ),
        out_shape=jax.ShapeDtypeStruct((TEAM, packed, LANES), jnp.bfloat16),
        compiler_params=pltpu.CompilerParams(vmem_limit_bytes=58 * 1024 * 1024),
        name="attend",
    )(slots, live, queries, state)


def exchange(block, mask, axis, count):
    return lax.ppermute(block, axis, [(i, i ^ mask) for i in range(count)])


def far_stage(held, one, two, count):
    from_one = exchange(held, one, "img", count)
    from_two = exchange(held, two, "img", count)
    opposite = exchange(from_one, two, "img", count)
    return [held, from_one, from_two, opposite]


def body(tokens, norm_gain, caption, null_caption, keep, bucket_rows, w_qkv):
    grid_rows, grid_cols, features_count = tokens.shape[1:]
    token_count = grid_rows * grid_cols
    seq_size = lax.axis_size("seq")
    img_size = lax.axis_size("img")
    side = 4
    teams = seq_size // TEAM
    seq_at = lax.axis_index("seq")
    img_at = lax.axis_index("img")
    rank = seq_at % TEAM
    same_rank = [[TEAM * j + r for j in range(teams)] for r in range(TEAM)]
    team = [[TEAM * j + r for r in range(TEAM)] for j in range(teams)]
    x_groups = [[y * side + x for x in range(side)] for y in range(side)]
    y_groups = [[y * side + x for y in range(side)] for x in range(side)]
    depth = features_count // img_size
    padded = -(-depth // 16) * 16
    columns = w_qkv.shape[1] * seq_size
    inner = columns // 3
    share = inner // TEAM
    main = share // LANES * LANES

    gathered = lax.all_gather(w_qkv, "seq", axis=0)
    wide = 2 * main + LANES
    first, second = pl.pallas_call(
        functools.partial(layout_kernel, layout_plan(w_qkv.shape[1], inner, share, main)),
        in_specs=[SMEM, VMEM],
        out_specs=[VMEM, VMEM],
        out_shape=[
            jax.ShapeDtypeStruct((side, padded, wide), jnp.bfloat16),
            jax.ShapeDtypeStruct((side, padded, main + LANES), jnp.bfloat16),
        ],
        compiler_params=pltpu.CompilerParams(vmem_limit_bytes=58 * 1024 * 1024),
        name="layout",
    )(rank.reshape(1).astype(jnp.int32), gathered)
    first, tokens = lax.optimization_barrier((first, tokens))
    first_near = lax.all_to_all(first, "img", 0, 0, axis_index_groups=x_groups)
    y_at, x_at = img_at // side, img_at % side
    place = jnp.concatenate(
        [
            jnp.bitwise_xor(y_at, FAR_MASKS) * side + NEAR_SLOTS,
            NEAR_SLOTS * side + jnp.bitwise_xor(x_at, FAR_MASKS),
        ]
    ).astype(jnp.int32)
    slots = jnp.bitwise_xor(rank, jnp.arange(TEAM, dtype=jnp.int32))
    first_row = (seq_at - rank + slots) * grid_rows
    live = jnp.clip(bucket_rows[0] - first_row, 0, grid_rows) * grid_cols
    second, first_near, place, live, slots = lax.optimization_barrier(
        (second, first_near, place, live, slots)
    )
    second_near = lax.all_to_all(second, "img", 0, 0, axis_index_groups=y_groups)
    first_pieces = far_stage(first_near, side, 3 * side, img_size)
    second_pieces = far_stage(second_near, 1, 3, img_size)
    features = jnp.transpose(tokens[0], (0, 2, 1)).astype(jnp.float32)
    mean_square = jnp.mean(features * features, axis=1, keepdims=True)
    condition = jnp.where(keep[0] > 0, caption[0], null_caption).astype(jnp.float32)
    hidden = (
        features * lax.rsqrt(mean_square + norm_eps) * norm_gain.astype(jnp.float32)[None, :, None]
        + condition[None, :, None]
    ).astype(jnp.bfloat16)
    hidden = hidden.reshape(grid_rows, img_size, depth, grid_cols)
    hidden = jnp.pad(hidden, ((0, 0), (0, 0), (0, padded - depth), (0, 0)))
    hidden = hidden.reshape(grid_rows, img_size * padded, grid_cols)
    mine = jnp.transpose(hidden, (0, 2, 1)).reshape(token_count, img_size * padded)
    beside = exchange(mine, 2, "seq", seq_size)
    late, _ = lax.optimization_barrier((beside, first_pieces[1:3]))
    across = exchange(late, 1, "seq", seq_size)
    hidden = (mine, exchange(mine, 1, "seq", seq_size), beside, across)

    part = compute_state(place, live, hidden, first_pieces, 1)
    part = jnp.broadcast_to(part, (teams,) + part.shape[1:])
    state = lax.all_to_all(part, "seq", 0, 0, axis_index_groups=same_rank)
    queries = compute_queries(place, hidden, second_pieces)

    result = compute_output(slots, live, queries, state)
    result = lax.all_to_all(result, "seq", 0, 0, axis_index_groups=team)
    result = pl.pallas_call(
        assemble_kernel,
        in_specs=[VMEM],
        out_specs=VMEM,
        out_shape=jax.ShapeDtypeStruct((token_count, inner), jnp.bfloat16),
        compiler_params=pltpu.CompilerParams(vmem_limit_bytes=16 * 1024 * 1024),
        name="assemble",
    )(result)
    return result.reshape(1, grid_rows, grid_cols, inner)


def solution(mesh):
    in_specs = (
        P("img", "seq", None, None),
        P(),
        P("img", None),
        P(),
        P("img"),
        P("img"),
        P("img", "seq"),
    )
    out_specs = P("img", "seq", None, None)

    return jax.shard_map(body, mesh=mesh, in_specs=in_specs, out_specs=out_specs, check_vma=False)
```
